512 devices in a mesh: prow: 16 (over x, z_hi), pcol: 32 (over z_lo, y, core).
Axes of the slice: x: 4, y: 8, z: 8 (z_hi: 4, z_lo: 2; z = z_hi * 2 + z_lo), core: 2. Of those that a mesh axis runs over, the one named last changes fastest.
Arguments:
- ancestor_inverse: bfloat16 [24576, 24576], P('pcol', 'prow'), may hold values from -6 to 6
- lower_panel: bfloat16 [24576, 1024], P(('prow', 'pcol')), may hold values from -0.3125 to 0.3125
- pivot_inverse: float32 [256, 1024], P('pcol', 'prow'), may hold values from -6 to 6
- struct_list: int32 [4, 48], replicated, may hold values from -1 to 95, as said below
Outputs:
- off_inverse: bfloat16 [24576, 1024], P('pcol', 'prow')
- diag_inverse: float32 [256, 1024], P('pcol', 'prow')
The draws below stay inside these ranges and needn't reach their ends.
Inputs may be any that keep to these rules, and one draw needn't show every extreme that they name: `struct_list`: each row lists distinct ancestor supernodes first, all within 48 cyclically consecutive ancestor numbers, then entries -1; every row has at least one ancestor and some row lists 48.
All inputs are finite; a program needn't handle non-finite values.
Results may differ from the reference program's by a relative error of at most 0.001.
Values may be sent and summed in bfloat16 or wider, within the bound.
A program may use at most 64 MiB of HBM per device.

```python
import jax
import jax.numpy as jnp
from jax import lax

B = 256
NK = 4
NA = 96
SLOTS = 48
GROUP = 6


def draw_struct_list(key, part):
    key_start, key_kept = jax.random.split(jax.random.fold_in(key, 11))
    window_start = jax.random.randint(key_start, (NK, 1), 0, NA)
    retained = jax.random.randint(key_kept, (NK, SLOTS), 0, 4) > 0
    offsets = jnp.arange(SLOTS, dtype=jnp.int32)[None, :]
    row_ids = jnp.arange(NK, dtype=jnp.int32)[:, None]
    retained = retained | (offsets == 0) | (row_ids == 0)
    ancestor_ids = (window_start + offsets) % NA
    sort_key = jnp.where(retained, offsets, offsets + SLOTS)
    ranking = jnp.argsort(sort_key, axis=1, stable=True)
    ids_sorted = jnp.take_along_axis(ancestor_ids, ranking, 1)
    kept_sorted = jnp.take_along_axis(retained, ranking, 1)
    return jnp.where(kept_sorted, ids_sorted, -1).astype(jnp.int32)


def with_spikes(drawn, own_key, source, target, parts, factor):
    def block_of(axis_at):
        return (jnp.arange(drawn.shape[axis_at]) // (drawn.shape[axis_at] // parts)).reshape((-1,) + (1,) * (drawn.ndim - 1 - axis_at))

    near = jax.random.permutation(own_key, parts)[block_of(target)]
    second = (block_of(target) + parts // 2) % parts
    return jnp.where((block_of(source) == near) | (block_of(source) == second), factor * drawn, drawn)


def block_scale(stream_key, shape, cuts, low, high):
    def one(position, shards_of):
        draws = jax.random.uniform(jax.random.fold_in(jax.random.fold_in(stream_key, 6), position), (shards_of,), jnp.float32, low / len(cuts), high / len(cuts))
        return jnp.repeat(jnp.exp(draws), shape[position] // shards_of).reshape((-1,) + (1,) * (len(shape) - position - 1))

    factor_of = one(*cuts[0])
    for cut in cuts[1:]:
        factor_of = factor_of * one(*cut)
    return factor_of


def centred(key, dims, deviation, limit, pieces=(), kind=jnp.bfloat16):
    loudness = block_scale(key, dims, pieces, -0.22, 0.18) if pieces else 1.0
    values = jax.random.normal(key, dims, jnp.float32) * deviation * loudness
    return jnp.minimum(jnp.maximum(values, -limit), limit).astype(kind)


def gaussian_with(key, dims, scale, limit, cuts, heavy, kind=jnp.bfloat16):
    entries = scale * jax.random.normal(key, dims, jnp.float32)
    if cuts:
        entries = entries * block_scale(key, dims, cuts, -0.22, 0.18)
    return jnp.clip(with_spikes(entries, jax.random.fold_in(key, 3), *heavy), -limit, limit).astype(kind)


def setup_inputs(seed: int = 0) -> dict:
    key_list = jax.random.split(jax.random.key(seed), 5)
    ancestor_inverse = centred(key_list[0], (NA * B, NA * B), 1.0, 6.0, ((0, 32), (1, 16)))
    lower_panel = gaussian_with(key_list[1], (NA * B, NK * B), (NA * B // 4) ** -0.5, 0.3125, ((0, 512),), (0, 1, 512, 6.0))
    pivot_inverse = centred(key_list[2], (B, NK * B), 1.0, 6.0, ((0, 32), (1, 16)), jnp.float32)
    struct_list = draw_struct_list(jax.random.fold_in(key_list[4], 71), 0)
    return {"ancestor_inverse": ancestor_inverse, "lower_panel": lower_panel, "pivot_inverse": pivot_inverse, "struct_list": struct_list}


def block_mask_of(struct_list):
    ancestors = jnp.arange(NA, dtype=jnp.int32)
    listed = struct_list[:, :, None] == ancestors[None, None, :]
    member = jnp.transpose(jnp.any(listed, axis=1)).astype(jnp.float32)
    return jnp.repeat(jnp.repeat(member, B, axis=0), B, axis=1)


def reference(ancestor_inverse, lower_panel, pivot_inverse, struct_list):
    block_mask = block_mask_of(struct_list)
    masked_lower = (lower_panel.astype(jnp.float32) * block_mask).astype(jnp.bfloat16)
    width = GROUP * B

    def add_group(group, total):
        columns = lax.dynamic_slice_in_dim(ancestor_inverse, group * width, width, 1)
        rows_part = lax.dynamic_slice_in_dim(masked_lower, group * width, width, 0)
        product = -jnp.dot(columns, rows_part, preferred_element_type=jnp.float32)
        return total + product

    summed = lax.fori_loop(0, NA // GROUP, add_group, jnp.zeros((NA * B, NK * B), jnp.float32))
    off_sum = summed * block_mask
    off_inverse = off_sum.astype(jnp.bfloat16)
    lower_blocks = masked_lower.astype(jnp.float32).reshape(NA * B, NK, B)
    off_blocks = off_sum.reshape(NA * B, NK, B)
    diag_term = jnp.einsum("ikr,ikc->rkc", lower_blocks, off_blocks, precision=lax.Precision.HIGHEST).reshape(B, NK * B)
    diag_inverse = pivot_inverse - diag_term
    return off_inverse, diag_inverse
```

```python
import jax
import jax.numpy as jnp
from jax import lax
from jax.experimental import pallas as pl
from jax.experimental.pallas import tpu as pltpu
from jax.sharding import PartitionSpec as P

B = 256
NK = 4
MESH = pl.DeviceIdType.MESH
F32 = jnp.float32
BF16 = jnp.bfloat16
ROWS = 48
SHARES = 16


def remote(src, dst, send, recv, device):
    return pltpu.make_async_remote_copy(
        src_ref=src, dst_ref=dst, send_sem=send, recv_sem=recv, device_id=device, device_id_type=MESH
    )


def kernel(
    mask,
    inverse,
    lower,
    pivot,
    off_out,
    diag_out,
    gathered,
    masked,
    own_rows,
    part,
    x_in,
    z_part,
    z_in,
    diag_part,
    diag_in,
    local_sem,
    pair_sem,
    ring_send,
    ring_recv,
    core_send,
    core_recv,
    rows_send,
    rows_recv,
    x_send,
    x_recv,
    z_send,
    z_recv,
    diag_send,
    diag_recv,
):
    r, c = lax.axis_index("prow"), lax.axis_index("pcol")
    x, zh = r // 4, r % 4
    zl, y, core = c // 16, (c % 16) // 2, c % 2
    target_col = 2 * r + c // SHARES
    slot = c % SHARES
    source_row = c // 2
    source_col = (c % 2) * SHARES
    self_rows = target_col == c

    def col_device(z_lo, y_at, core_at):
        return {"prow": r, "pcol": z_lo * 16 + y_at * 2 + core_at}

    def x_device(step):
        return {"prow": ((x + step + 4) % 4) * 4 + zh, "pcol": c}

    def z_device(step):
        return {"prow": x * 4 + (zh + step + 4) % 4, "pcol": c}

    barrier = pltpu.get_barrier_semaphore()

    @pl.loop(1, 32)
    def _(i):
        pl.semaphore_signal(
            barrier, inc=1, device_id={"prow": r, "pcol": (c + i) % 32}, device_id_type=MESH
        )

    for device in (x_device(1), x_device(-1), z_device(1), z_device(-1)):
        pl.semaphore_signal(barrier, inc=1, device_id=device, device_id_type=MESH)

    @pl.loop(0, SHARES)
    def _(s):
        @pl.when(jnp.logical_not((source_row == r) & (source_col + s == c)))
        def _():
            pl.semaphore_signal(
                barrier,
                inc=1,
                device_id={"prow": source_row, "pcol": source_col + s},
                device_id_type=MESH,
            )

    pl.semaphore_wait(barrier, 35 + SHARES - self_rows.astype(jnp.int32))

    def shard(z_lo, y_at, core_at):
        at = (z_lo * 16 + y_at * 2 + core_at) * ROWS
        return gathered.at[pl.ds(pl.multiple_of(at, 16), ROWS)]

    sent = []
    core_copies = []

    def to_core(src, dst):
        n = len(core_copies)
        copy = remote(src, dst, core_send.at[n], core_recv.at[n], col_device(zl, y, 1 - core))
        copy.start()
        core_copies.append(copy)

    ring = {}

    def to_ring(chain, way, step, src, dst):
        n = (chain * 2 + way) * 4 + step
        device = col_device(zl, (y + (1 if way == 0 else 7)) % 8, core)
        copy = remote(src, dst, ring_send.at[n], ring_recv.at[n], device)
        copy.start()
        ring[chain, way, step] = copy

    mine = shard(zl, y, core)
    pair = remote(lower, mine, pair_sem.at[0], pair_sem.at[1], col_device(1 - zl, y, core))
    pair.start()
    to_ring(0, 0, 0, lower, mine)
    to_ring(0, 1, 0, lower, mine)
    to_core(lower, mine)
    keep = pltpu.make_async_copy(lower, mine, local_sem)
    keep.start()
    pair.wait_recv()
    theirs = shard(1 - zl, y, core)
    to_ring(1, 0, 0, theirs, theirs)
    to_ring(1, 1, 0, theirs, theirs)
    to_core(theirs, theirs)
    for step in range(1, 5):
        for chain in range(2):
            for way in range(2):
                if (chain, way, step - 1) not in ring:
                    continue
                ring[chain, way, step - 1].wait_recv()
                origin = (y + (8 - step if way == 0 else step)) % 8
                piece = shard(zl if chain == 0 else 1 - zl, origin, core)
                if step < 3 or (step == 3 and chain == way):
                    to_ring(chain, way, step, piece, piece)
                to_core(piece, piece)

    def rows_copy(i):
        row = (r + i) % 16
        columns = pl.ds(pl.multiple_of((row // 4) * B, B), B)
        return remote(
            lower.at[:, columns],
            own_rows.at[pl.ds(pl.multiple_of(slot * ROWS, 16), ROWS)],
            rows_send.at[i],
            rows_recv.at[slot],
            {"prow": row, "pcol": target_col},
        )

    @pl.loop(1, 16)
    def _(i):
        rows_copy(i).start()

    @pl.when(jnp.logical_not(self_rows))
    def _():
        rows_copy(0).start()

    @pl.when(self_rows)
    def _():
        columns = pl.ds(pl.multiple_of(x * B, B), B)
        own_rows[pl.ds(pl.multiple_of(slot * ROWS, 16), ROWS), :] = lower[:, columns]

    keep.wait()
    for copy in core_copies:
        copy.wait_recv()

    @pl.loop(0, 6)
    def _(j):
        rows = pl.ds(pl.multiple_of(j * B, B), B)
        for k in range(NK):
            columns = pl.ds(k * B, B)
            value = gathered[rows, columns].astype(F32) * mask[j * NK + k]
            masked[rows, columns] = value.astype(BF16)

    def multiply(k):
        columns = pl.ds(pl.multiple_of(k * B, B), B)

        @pl.loop(0, 2)
        def _(half):
            rows = pl.ds(pl.multiple_of(half * 384, 128), 384)
            part[k, half] = jnp.dot(
                inverse[rows, :], masked[:, columns], preferred_element_type=F32
            )

    def hop(source, target, n, sends, recvs, device):
        copy = remote(source, target.at[n], sends.at[n], recvs.at[n], device)
        copy.start()
        sent.append(copy)
        return copy

    far, ahead, behind = (x + 2) % 4, (x + 1) % 4, (x + 3) % 4
    multiply(far)
    mid_up = hop(part.at[far, 0], x_in, 0, x_send, x_recv, x_device(1))
    mid_down = hop(part.at[far, 1], x_in, 1, x_send, x_recv, x_device(-1))
    multiply(ahead)
    raw_up = hop(part.at[ahead, 1], x_in, 2, x_send, x_recv, x_device(1))
    multiply(behind)
    raw_down = hop(part.at[behind, 0], x_in, 4, x_send, x_recv, x_device(-1))
    multiply(x)
    mid_up.wait_recv()
    part[ahead, 0] = part[ahead, 0] + x_in[0]
    sum_up = hop(part.at[ahead, 0], x_in, 3, x_send, x_recv, x_device(1))
    mid_down.wait_recv()
    part[behind, 1] = part[behind, 1] + x_in[1]
    sum_down = hop(part.at[behind, 1], x_in, 5, x_send, x_recv, x_device(-1))
    raw_up.wait_recv()
    raw_down.wait_recv()
    part[x, 0] = part[x, 0] + x_in[4]
    part[x, 1] = part[x, 1] + x_in[2]
    sum_up.wait_recv()
    sum_down.wait_recv()

    for h in range(4):
        lanes = slice(64 * h, 64 * h + 64)
        for half in range(2):
            rows = pl.ds(half * 192, 192)
            low = part[x, 0, rows, lanes] + x_in[3, rows, lanes]
            high = part[x, 1, rows, lanes] + x_in[5, rows, lanes]
            z_part[h, half] = jnp.concatenate([low, high], axis=1)

    far, ahead, behind = (zh + 2) % 4, (zh + 1) % 4, (zh + 3) % 4
    mid_up = hop(z_part.at[far, 0], z_in, 0, z_send, z_recv, z_device(1))
    mid_down = hop(z_part.at[far, 1], z_in, 1, z_send, z_recv, z_device(-1))
    raw_up = hop(z_part.at[ahead, 1], z_in, 2, z_send, z_recv, z_device(1))
    raw_down = hop(z_part.at[behind, 0], z_in, 4, z_send, z_recv, z_device(-1))
    mid_up.wait_recv()
    z_part[ahead, 0] = z_part[ahead, 0] + z_in[0]
    sum_up = hop(z_part.at[ahead, 0], z_in, 3, z_send, z_recv, z_device(1))
    mid_down.wait_recv()
    z_part[behind, 1] = z_part[behind, 1] + z_in[1]
    sum_down = hop(z_part.at[behind, 1], z_in, 5, z_send, z_recv, z_device(-1))

    @pl.loop(0, SHARES)
    def _(s):
        @pl.when(jnp.logical_not((source_row == r) & (source_col + s == c)))
        def _():
            here = own_rows.at[pl.ds(pl.multiple_of(s * ROWS, 16), ROWS)]
            remote(here, here, rows_send.at[0], rows_recv.at[s], x_device(1)).wait_recv()

    raw_up.wait_recv()
    raw_down.wait_recv()
    sum_up.wait_recv()
    sum_down.wait_recv()
    lane = lax.broadcasted_iota(jnp.int32, (192, 128), 1)
    row = lax.broadcasted_iota(jnp.int32, (192, 128), 0) + jnp.where(lane < 64, 0, 384)
    upper = jnp.zeros((B, 128), F32)
    lower_half = jnp.zeros((B, 128), F32)
    for half in range(2):
        at = row + half * 192
        keep_row = jnp.where(at < B, mask[24], jnp.where(at < 2 * B, mask[25], mask[26]))
        first, second = (3, 4) if half == 0 else (5, 2)
        total = (z_part[zh, half] + z_in[first] + z_in[second]) * keep_row
        off_out[pl.ds(half * 192, 192), :] = total[:, :64].astype(BF16)
        off_out[pl.ds(384 + half * 192, 192), :] = total[:, 64:].astype(BF16)
        big = total.astype(BF16)
        small = (total - big.astype(F32)).astype(BF16)
        left = own_rows[pl.ds(half * 192, 192), :]
        right = own_rows[pl.ds(384 + half * 192, 192), :]
        over_rows = (((0,), (0,)), ((), ()))
        for piece in (big, small):
            upper = upper + lax.dot_general(left, piece, over_rows, preferred_element_type=F32)
            lower_half = lower_half + lax.dot_general(
                right, piece, over_rows, preferred_element_type=F32
            )
    lane = lax.broadcasted_iota(jnp.int32, (B, 128), 1)
    diag_part[...] = jnp.where(lane < 64, upper, lower_half)

    def diag_copy(i):
        to = (c + i) % 32
        return remote(
            diag_part.at[pl.ds(pl.multiple_of(to * 8, 8), 8)],
            diag_in.at[c],
            diag_send.at[i],
            diag_recv.at[c],
            {"prow": r, "pcol": to},
        )

    @pl.loop(1, 32)
    def _(i):
        diag_copy(i).start()

    diag_in[c] = diag_part[pl.ds(pl.multiple_of(c * 8, 8), 8), :]

    pair.wait_send()
    for copy in list(ring.values()) + core_copies + sent:
        copy.wait_send()

    @pl.loop(1, 16)
    def _(i):
        rows_copy(i).wait_send()

    @pl.when(jnp.logical_not(self_rows))
    def _():
        rows_copy(0).wait_send()

    @pl.loop(1, 32)
    def _(i):
        diag_copy(i).wait_send()
        source = (c + i) % 32
        here = diag_in.at[source]
        remote(here, here, diag_send.at[0], diag_recv.at[source], x_device(1)).wait_recv()

    term = jnp.sum(diag_in[...], axis=0)
    diag_out[...] = pivot[...] - (term[:, :64] + term[:, 64:])


def body(ancestor_inverse, lower_panel, pivot_inverse, struct_list):
    r, c = lax.axis_index("prow"), lax.axis_index("pcol")
    col_ids = r * 6 + jnp.arange(6, dtype=jnp.int32)
    row_ids = c * 3 + jnp.arange(3, dtype=jnp.int32)
    cols = jnp.any(struct_list[None, :, :] == col_ids[:, None, None], axis=2)
    level = lax.dynamic_slice_in_dim(struct_list, r // 4, 1, 0)
    rows = jnp.any(level == row_ids[:, None], axis=1)
    mask = jnp.concatenate(
        [-cols.astype(F32).reshape(24), rows.astype(F32), jnp.zeros((5,), F32)]
    )
    vmem = pl.BlockSpec(memory_space=pltpu.VMEM)
    dma = pltpu.SemaphoreType.DMA
    return pl.pallas_call(
        kernel,
        out_shape=(
            jax.ShapeDtypeStruct((768, 64), BF16),
            jax.ShapeDtypeStruct((8, 64), F32),
        ),
        in_specs=[pl.BlockSpec(memory_space=pltpu.SMEM), vmem, vmem, vmem],
        out_specs=(vmem, vmem),
        scratch_shapes=[
            pltpu.VMEM((1536, 1024), BF16),
            pltpu.VMEM((1536, 1024), BF16),
            pltpu.VMEM((768, B), BF16),
            pltpu.VMEM((4, 2, 384, B), F32),
            pltpu.VMEM((6, 384, B), F32),
            pltpu.VMEM((4, 2, 192, 128), F32),
            pltpu.VMEM((6, 192, 128), F32),
            pltpu.VMEM((B, 128), F32),
            pltpu.VMEM((32, 8, 128), F32),
            dma,
            dma((2,)),
            dma((16,)),
            dma((16,)),
            dma((16,)),
            dma((16,)),
            dma((16,)),
            dma((16,)),
            dma((6,)),
            dma((6,)),
            dma((6,)),
            dma((6,)),
            dma((32,)),
            dma((32,)),
        ],
        compiler_params=pltpu.CompilerParams(
            collective_id=0, has_side_effects=True, vmem_limit_bytes=48 * 1024 * 1024
        ),
    )(mask, ancestor_inverse, lower_panel, pivot_inverse)


def solution(mesh):
    placed = (P("pcol", "prow"), P(("prow", "pcol"), None), P("pcol", "prow"), P())
    return jax.shard_map(
        body,
        mesh=mesh,
        in_specs=placed,
        out_specs=(P("pcol", "prow"), P("pcol", "prow")),
        check_vma=False,
    )
```

```python
import jax
import jax.numpy as jnp
from jax import lax
from jax.experimental import pallas as pl
from jax.experimental.pallas import tpu as pltpu
from jax.sharding import PartitionSpec as P

B = 256
NK = 4
MESH = pl.DeviceIdType.MESH
F32 = jnp.float32
BF16 = jnp.bfloat16
ROWS = 48
SHARES = 16
CHUNKS = 2
CHUNK = 384 // CHUNKS


def remote(src, dst, send, recv, device):
    return pltpu.make_async_remote_copy(
        src_ref=src, dst_ref=dst, send_sem=send, recv_sem=recv, device_id=device, device_id_type=MESH
    )


def kernel(
    lists,
    inverse_hbm,
    lower,
    pivot_hbm,
    off_out,
    diag_out,
    inverse,
    pivot,
    gathered,
    masked,
    row_in,
    own_rows,
    part,
    x_in,
    z_part,
    z_in,
    core_part,
    core_in,
    pair_part,
    pair_in,
    y_part,
    y_in,
    local_sem,
    pair_sem,
    ring_send,
    ring_recv,
    core_send,
    core_recv,
    row_sem,
    slice_send,
    slice_recv,
    band_send,
    band_recv,
    x_send,
    x_recv,
    z_send,
    z_recv,
    sum_sem,
    y_send,
    y_recv,
):
    r, c = lax.axis_index("prow"), lax.axis_index("pcol")
    x, zh = r // 4, r % 4
    zl, y, core = c // 16, (c % 16) // 2, c % 2
    share = zh * 4 + x
    source = {"prow": c // 2, "pcol": (c % 2) * SHARES + share}
    target_row, target_col = (c % 4) * 4 + (c % SHARES) // 4, 2 * r + c // SHARES
    stays = (target_row == r) & (target_col == c)

    def col_device(z_lo, y_at, core_at):
        return {"prow": r, "pcol": z_lo * 16 + (y_at % 8) * 2 + core_at}

    def x_device(step):
        return {"prow": ((x + step + 4) % 4) * 4 + zh, "pcol": c}

    def z_device(step):
        return {"prow": x * 4 + (zh + step + 4) % 4, "pcol": c}

    big_copy = pltpu.make_async_copy(inverse_hbm, inverse, local_sem.at[1])
    big_copy.start()
    pivot_copy = pltpu.make_async_copy(pivot_hbm, pivot, local_sem.at[2])
    pivot_copy.start()

    barrier = pltpu.get_barrier_semaphore()
    friends = [col_device(zl, y + i, core) for i in range(1, 8)]
    friends += [col_device(zl, y, 1 - core), col_device(1 - zl, y, core)]
    friends += [x_device(1), x_device(2), x_device(3), z_device(1), z_device(-1)]
    for device in friends:
        pl.semaphore_signal(barrier, inc=1, device_id=device, device_id_type=MESH)

    @pl.when(jnp.logical_not(stays))
    def _():
        pl.semaphore_signal(barrier, inc=1, device_id=source, device_id_type=MESH)

    pl.semaphore_wait(barrier, len(friends) + 1 - stays.astype(jnp.int32))

    def shard(z_lo, y_at, core_at):
        at = (z_lo * 16 + y_at * 2 + core_at) * ROWS
        return gathered.at[pl.ds(pl.multiple_of(at, 16), ROWS)]

    sent = []
    core_copies = []

    def send(src, dst, send_sem, recv_sem, device):
        copy = remote(src, dst, send_sem, recv_sem, device)
        copy.start()
        sent.append(copy)
        return copy

    def to_core(src, dst):
        n = len(core_copies)
        core_copies.append(
            send(src, dst, core_send.at[n], core_recv.at[n], col_device(zl, y, 1 - core))
        )

    ring = {}

    def to_ring(chain, way, step, src, dst):
        n = (chain * 2 + way) * 4 + step
        device = col_device(zl, y + (1 if way == 0 else 7), core)
        ring[chain, way, step] = send(src, dst, ring_send.at[n], ring_recv.at[n], device)

    mine = shard(zl, y, core)
    pair = send(lower, mine, pair_sem.at[0], pair_sem.at[1], col_device(1 - zl, y, core))
    to_ring(0, 0, 0, lower, mine)
    to_ring(0, 1, 0, lower, mine)
    to_core(lower, mine)
    keep = pltpu.make_async_copy(lower, mine, local_sem.at[0])
    keep.start()
    row_copy = remote(
        lower, row_in, row_sem.at[0], row_sem.at[1], {"prow": target_row, "pcol": target_col}
    )
    row_keep = pltpu.make_async_copy(lower, row_in, row_sem.at[2])

    @pl.when(jnp.logical_not(stays))
    def _():
        row_copy.start()

    @pl.when(stays)
    def _():
        row_keep.start()

    pair.wait_recv()
    theirs = shard(1 - zl, y, core)
    to_ring(1, 0, 0, theirs, theirs)
    to_ring(1, 1, 0, theirs, theirs)
    to_core(theirs, theirs)
    for step in range(1, 5):
        for chain in range(2):
            for way in range(2):
                if (chain, way, step - 1) not in ring:
                    continue
                ring[chain, way, step - 1].wait_recv()
                origin = (y + (8 - step if way == 0 else step)) % 8
                piece = shard(zl if chain == 0 else 1 - zl, origin, core)
                if step < 3 or (step == 3 and chain == way):
                    to_ring(chain, way, step, piece, piece)
                to_core(piece, piece)

    @pl.when(jnp.logical_not(stays))
    def _():
        row_copy.wait_recv()

    @pl.when(stays)
    def _():
        row_keep.wait()

    def columns_of(k):
        return pl.ds(pl.multiple_of(k * B, B), B)

    def band(at, size):
        return own_rows.at[pl.ds(pl.multiple_of(at, 16), size)]

    slices = [
        send(
            row_in.at[:, columns_of((x + i) % 4)],
            band(share * ROWS, ROWS),
            slice_send.at[i - 1],
            slice_recv.at[i - 1],
            x_device(i),
        )
        for i in (1, 3, 2)
    ]
    slice_keep = pltpu.make_async_copy(
        row_in.at[:, columns_of(x)], band(share * ROWS, ROWS), local_sem.at[3]
    )
    slice_keep.start()
    keep.wait()
    big_copy.wait()
    for copy in core_copies:
        copy.wait_recv()

    for j in range(6):
        rows = pl.ds(j * B, B)
        listed = jnp.max(jnp.where(lists[...] == r * 6 + j, 1.0, 0.0), axis=1, keepdims=True)
        for k in range(NK):
            columns = pl.ds(k * B, B)
            value = gathered[rows, columns].astype(F32) * -listed[k : k + 1, :]
            masked[rows, columns] = value.astype(BF16)

    def multiply(k):
        columns = columns_of(k)

        @pl.loop(0, 2)
        def _(half):
            rows = pl.ds(pl.multiple_of(half * 384, 128), 384)
            product = jnp.dot(inverse[rows, :], masked[:, columns], preferred_element_type=F32)
            part[k, half] = product.reshape(CHUNKS, CHUNK, B)

    def hop(source, target, sends, recvs, chunk, n, device):
        at = chunk * 6 + n
        return send(source, target.at[chunk, n], sends.at[at], recvs.at[at], device)

    far, ahead, behind = (x + 2) % 4, (x + 1) % 4, (x + 3) % 4
    hops = {}

    def x_mid(h):
        hops["x", h, 0] = hop(part.at[far, 0, h], x_in, x_send, x_recv, h, 0, x_device(1))
        hops["x", h, 1] = hop(part.at[far, 1, h], x_in, x_send, x_recv, h, 1, x_device(-1))

    def x_raw_up(h):
        hops["x", h, 2] = hop(part.at[ahead, 1, h], x_in, x_send, x_recv, h, 2, x_device(1))

    def x_raw_down(h):
        hops["x", h, 4] = hop(part.at[behind, 0, h], x_in, x_send, x_recv, h, 4, x_device(-1))

    def x_sum(h):
        hops["x", h, 0].wait_recv()
        part[ahead, 0, h] = part[ahead, 0, h] + x_in[h, 0]
        hops["x", h, 3] = hop(part.at[ahead, 0, h], x_in, x_send, x_recv, h, 3, x_device(1))
        hops["x", h, 1].wait_recv()
        part[behind, 1, h] = part[behind, 1, h] + x_in[h, 1]
        hops["x", h, 5] = hop(part.at[behind, 1, h], x_in, x_send, x_recv, h, 5, x_device(-1))

    z_far, z_ahead, z_behind = (zh + 2) % 4, (zh + 1) % 4, (zh + 3) % 4

    def z_start(h):
        for n in (2, 3, 4, 5):
            hops["x", h, n].wait_recv()
        for way in range(2):
            rows = pl.ds(way * (CHUNK // 2), CHUNK // 2)
            low = part[x, 0, h, rows, :] + x_in[h, 3, rows, :] + x_in[h, 4, rows, :]
            high = part[x, 1, h, rows, :] + x_in[h, 5, rows, :] + x_in[h, 2, rows, :]
            for q in range(4):
                lanes = slice(64 * q, 64 * q + 64)
                z_part[q, h, way] = jnp.concatenate([low[:, lanes], high[:, lanes]], axis=1)
        up, down = z_device(1), z_device(-1)
        hops["z", h, 0] = hop(z_part.at[z_far, h, 0], z_in, z_send, z_recv, h, 0, up)
        hops["z", h, 1] = hop(z_part.at[z_far, h, 1], z_in, z_send, z_recv, h, 1, down)
        hops["z", h, 2] = hop(z_part.at[z_ahead, h, 1], z_in, z_send, z_recv, h, 2, up)
        hops["z", h, 4] = hop(z_part.at[z_behind, h, 0], z_in, z_send, z_recv, h, 4, down)

    def z_sum(h):
        hops["z", h, 0].wait_recv()
        z_part[z_ahead, h, 0] = z_part[z_ahead, h, 0] + z_in[h, 0]
        hops["z", h, 3] = hop(z_part.at[z_ahead, h, 0], z_in, z_send, z_recv, h, 3, z_device(1))
        hops["z", h, 1].wait_recv()
        z_part[z_behind, h, 1] = z_part[z_behind, h, 1] + z_in[h, 1]
        hops["z", h, 5] = hop(z_part.at[z_behind, h, 1], z_in, z_send, z_recv, h, 5, z_device(-1))

    def band_copy(n, at, size, device):
        here = band(at, size)
        return send(here, here, band_send.at[n], band_recv.at[n], device)

    multiply(far)
    x_mid(0)
    multiply(ahead)
    x_raw_up(0)
    multiply(behind)
    x_raw_down(0)
    if CHUNKS > 1:
        x_mid(1)
    slice_keep.wait()
    for copy in slices:
        copy.wait_recv()
    band_up = band_copy(0, zh * 192, 192, z_device(1))
    band_down = band_copy(1, zh * 192, 192, z_device(-1))
    multiply(x)
    far_up = far_down = None
    for h in range(CHUNKS):
        x_sum(h)
        if h + 1 < CHUNKS:
            x_raw_up(h + 1)
            x_raw_down(h + 1)
        if h + 2 < CHUNKS:
            x_mid(h + 2)
        if h == 0:
            band_up.wait_recv()
            far_up = band_copy(2, z_behind * 192, 96, z_device(1))
            band_down.wait_recv()
            far_down = band_copy(3, z_ahead * 192 + 96, 96, z_device(-1))
        if h >= 2:
            z_sum(h - 2)
        if h >= 1:
            z_start(h - 1)
    if CHUNKS > 1:
        z_sum(CHUNKS - 2)
    z_start(CHUNKS - 1)
    z_sum(CHUNKS - 1)
    far_up.wait_recv()
    far_down.wait_recv()

    half_rows = CHUNK // 2
    lane = lax.broadcasted_iota(jnp.int32, (half_rows, 128), 1)
    row = lax.broadcasted_iota(jnp.int32, (half_rows, 128), 0) + jnp.where(lane < 64, 0, 384)
    kept = [
        jnp.max(jnp.where(lists[...] == c * 3 + i, 1.0, 0.0), axis=1, keepdims=True)
        for i in range(3)
    ]
    level = lax.broadcasted_iota(jnp.int32, (NK, 1), 0) == x
    kept = [jnp.sum(jnp.where(level, k, 0.0), axis=0, keepdims=True) for k in kept]
    left_sum = jnp.zeros((B, 128), F32)
    right_sum = jnp.zeros((B, 128), F32)
    over_rows = (((0,), (0,)), ((), ()))
    for h in range(CHUNKS):
        for n in (2, 3, 4, 5):
            hops["z", h, n].wait_recv()
        for way in range(2):
            start = h * CHUNK + way * half_rows
            at = row + start
            keep_row = jnp.where(at < B, kept[0], jnp.where(at < 2 * B, kept[1], kept[2]))
            first, second = (3, 4) if way == 0 else (5, 2)
            total = (z_part[zh, h, way] + z_in[h, first] + z_in[h, second]) * keep_row
            off_out[pl.ds(start, half_rows), :] = total[:, :64].astype(BF16)
            off_out[pl.ds(384 + start, half_rows), :] = total[:, 64:].astype(BF16)
            big = total.astype(BF16)
            small = (total - big.astype(F32)).astype(BF16)
            left = own_rows[pl.ds(start, half_rows), :]
            right = own_rows[pl.ds(384 + start, half_rows), :]
            for piece in (big, small):
                left_sum = left_sum + lax.dot_general(
                    left, piece, over_rows, preferred_element_type=F32
                )
                right_sum = right_sum + lax.dot_general(
                    right, piece, over_rows, preferred_element_type=F32
                )
    lane = lax.broadcasted_iota(jnp.int32, (B, 128), 1)
    term = jnp.where(lane < 64, left_sum, right_sum).reshape(2, 8, 2, 8, 128)

    for q in range(2):
        core_part[q] = term[:, :, q]
    copy = send(
        core_part.at[1 - core], core_in, sum_sem.at[0], sum_sem.at[1], col_device(zl, y, 1 - core)
    )
    copy.wait_recv()
    pair_part[...] = core_part[core] + core_in[...]
    copy = send(
        pair_part.at[1 - zl], pair_in, sum_sem.at[2], sum_sem.at[3], col_device(1 - zl, y, core)
    )
    copy.wait_recv()
    y_part[...] = pair_part[zl] + pair_in[...]
    y_copies = [
        send(
            y_part.at[(y + i) % 8],
            y_in.at[i - 1],
            y_send.at[i - 1],
            y_recv.at[i - 1],
            col_device(zl, y + i, core),
        )
        for i in range(1, 8)
    ]
    pivot_copy.wait()
    total = y_part[y]
    for i, copy in enumerate(y_copies):
        copy.wait_recv()
        total = total + y_in[i]
    diag_out[...] = pivot[...] - (total[:, :64] + total[:, 64:])

    for copy in sent:
        copy.wait_send()

    @pl.when(jnp.logical_not(stays))
    def _():
        row_copy.wait_send()


def body(ancestor_inverse, lower_panel, pivot_inverse, struct_list):
    vmem = pl.BlockSpec(memory_space=pltpu.VMEM)
    hbm = pl.BlockSpec(memory_space=pltpu.HBM)
    dma = pltpu.SemaphoreType.DMA
    hop_sems = [dma((6 * CHUNKS,))] * 4
    return pl.pallas_call(
        kernel,
        out_shape=(
            jax.ShapeDtypeStruct((768, 64), BF16),
            jax.ShapeDtypeStruct((8, 64), F32),
        ),
        in_specs=[vmem, hbm, hbm, hbm],
        out_specs=(vmem, vmem),
        scratch_shapes=[
            pltpu.VMEM((768, 1536), BF16),
            pltpu.VMEM((8, 64), F32),
            pltpu.VMEM((1536, 1024), BF16),
            pltpu.VMEM((1536, 1024), BF16),
            pltpu.VMEM((48, 1024), BF16),
            pltpu.VMEM((768, B), BF16),
            pltpu.VMEM((4, 2, CHUNKS, CHUNK, B), F32),
            pltpu.VMEM((CHUNKS, 6, CHUNK, B), F32),
            pltpu.VMEM((4, CHUNKS, 2, CHUNK // 2, 128), F32),
            pltpu.VMEM((CHUNKS, 6, CHUNK // 2, 128), F32),
            pltpu.VMEM((2, 2, 8, 8, 128), F32),
            pltpu.VMEM((2, 8, 8, 128), F32),
            pltpu.VMEM((2, 8, 8, 128), F32),
            pltpu.VMEM((8, 8, 128), F32),
            pltpu.VMEM((8, 8, 128), F32),
            pltpu.VMEM((7, 8, 128), F32),
            dma((4,)),
            dma((2,)),
            dma((16,)),
            dma((16,)),
            dma((16,)),
            dma((16,)),
            dma((3,)),
            dma((3,)),
            dma((3,)),
            dma((4,)),
            dma((4,)),
            *hop_sems,
            dma((4,)),
            dma((7,)),
            dma((7,)),
        ],
        compiler_params=pltpu.CompilerParams(
            collective_id=0, has_side_effects=True
        ),
    )(struct_list, ancestor_inverse, lower_panel, pivot_inverse)


def solution(mesh):
    placed = (P("pcol", "prow"), P(("prow", "pcol"), None), P("pcol", "prow"), P())
    return jax.shard_map(
        body,
        mesh=mesh,
        in_specs=placed,
        out_specs=(P("pcol", "prow"), P("pcol", "prow")),
        check_vma=False,
    )
```

```python
import jax
import jax.numpy as jnp
from jax import lax
from jax.experimental import pallas as pl
from jax.experimental.pallas import tpu as pltpu
from jax.sharding import PartitionSpec as P

B = 256
NK = 4
MESH = pl.DeviceIdType.MESH
F32 = jnp.float32
BF16 = jnp.bfloat16
ROWS = 48
SHARES = 16
CHUNKS = 3
CHUNK = 384 // CHUNKS


def remote(src, dst, send, recv, device):
    return pltpu.make_async_remote_copy(
        src_ref=src, dst_ref=dst, send_sem=send, recv_sem=recv, device_id=device, device_id_type=MESH
    )


def kernel(
    lists,
    inverse_hbm,
    lower_hbm,
    pivot_hbm,
    off_out,
    diag_out,
    inverse,
    pivot,
    raw,
    lower,
    gathered,
    row_in,
    own_rows,
    part,
    x_in,
    z_part,
    z_in,
    core_part,
    core_in,
    y_part,
    y_in,
    local_sem,
    pair_sem,
    ring_send,
    ring_recv,
    core_send,
    core_recv,
    row_sem,
    slice_send,
    slice_recv,
    band_send,
    band_recv,
    x_send,
    x_recv,
    z_send,
    z_recv,
    sum_sem,
    y_send,
    y_recv,
):
    r, c = lax.axis_index("prow"), lax.axis_index("pcol")
    x, zh = r // 4, r % 4
    zl, y, core = c // 16, (c % 16) // 2, c % 2
    share = zh * 4 + x
    source = {"prow": c // 2, "pcol": (c % 2) * SHARES + share}
    target_row, target_col = (c % 4) * 4 + (c % SHARES) // 4, 2 * r + c // SHARES
    stays = (target_row == r) & (target_col == c)

    def col_device(z_lo, y_at, core_at):
        return {"prow": r, "pcol": z_lo * 16 + (y_at % 8) * 2 + core_at}

    def x_device(step):
        return {"prow": ((x + step + 4) % 4) * 4 + zh, "pcol": c}

    def z_device(step):
        return {"prow": x * 4 + (zh + step + 4) % 4, "pcol": c}

    big_copy = pltpu.make_async_copy(inverse_hbm, inverse, local_sem.at[1])
    big_copy.start()
    pivot_copy = pltpu.make_async_copy(pivot_hbm, pivot, local_sem.at[2])
    pivot_copy.start()

    raw_copy = pltpu.make_async_copy(lower_hbm, raw, local_sem.at[4])
    raw_copy.start()

    barrier = pltpu.get_barrier_semaphore()
    friends = [col_device(zl, y + i, core) for i in range(1, 8)]
    friends += [col_device(1 - zl, y + i, core) for i in range(8)] + [col_device(zl, y, 1 - core)]
    friends += [x_device(1), x_device(2), x_device(3), z_device(1), z_device(-1)]
    for device in friends:
        pl.semaphore_signal(barrier, inc=1, device_id=device, device_id_type=MESH)

    @pl.when(jnp.logical_not(stays))
    def _():
        pl.semaphore_signal(barrier, inc=1, device_id=source, device_id_type=MESH)

    def listed(ancestor):
        found = jnp.where(lists[...] == ancestor, 1.0, 0.0)
        return jnp.max(found, axis=1, keepdims=True)

    raw_copy.wait()
    begin = (r * 32 + c) * ROWS
    first = begin // B
    in_first = lax.broadcasted_iota(jnp.int32, (ROWS, B), 0) + begin < (first + 1) * B
    of_first, of_next = listed(first), listed(first + 1)
    for k in range(NK):
        columns = pl.ds(k * B, B)
        member = jnp.where(in_first, of_first[k : k + 1, :], of_next[k : k + 1, :])
        lower[:, columns] = (raw[:, columns].astype(F32) * member).astype(BF16)

    pl.semaphore_wait(barrier, len(friends) + 1 - stays.astype(jnp.int32))

    def shard(z_lo, y_at, core_at):
        at = (z_lo * 16 + y_at * 2 + core_at) * ROWS
        return gathered.at[pl.ds(pl.multiple_of(at, 16), ROWS)]

    sent = []
    core_copies = []

    def send(src, dst, send_sem, recv_sem, device):
        copy = remote(src, dst, send_sem, recv_sem, device)
        copy.start()
        sent.append(copy)
        return copy

    def to_core(src, dst):
        n = len(core_copies)
        core_copies.append(
            send(src, dst, core_send.at[n], core_recv.at[n], col_device(zl, y, 1 - core))
        )

    ring = {}

    def to_ring(chain, way, step, src, dst):
        n = (chain * 2 + way) * 4 + step
        device = col_device(zl, y + (1 if way == 0 else 7), core)
        ring[chain, way, step] = send(src, dst, ring_send.at[n], ring_recv.at[n], device)

    mine = shard(zl, y, core)
    pair = send(lower, mine, pair_sem.at[0], pair_sem.at[1], col_device(1 - zl, y, core))
    to_ring(0, 0, 0, lower, mine)
    to_ring(0, 1, 0, lower, mine)
    to_core(lower, mine)
    keep = pltpu.make_async_copy(lower, mine, local_sem.at[0])
    keep.start()
    row_copy = remote(
        lower, row_in, row_sem.at[0], row_sem.at[1], {"prow": target_row, "pcol": target_col}
    )
    row_keep = pltpu.make_async_copy(lower, row_in, row_sem.at[2])

    pair.wait_recv()
    theirs = shard(1 - zl, y, core)
    to_ring(1, 0, 0, theirs, theirs)
    to_ring(1, 1, 0, theirs, theirs)
    to_core(theirs, theirs)
    pair_copies = [pair]

    def to_pair(piece):
        n = len(pair_copies)
        pair_copies.append(
            send(piece, piece, pair_sem.at[2 * n], pair_sem.at[2 * n + 1], col_device(1 - zl, y, core))
        )

    for step in range(1, 5):
        for chain in range(2):
            for way in range(2):
                if (chain, way, step - 1) not in ring:
                    continue
                ring[chain, way, step - 1].wait_recv()
                origin = (y + (8 - step if way == 0 else step)) % 8
                piece = shard(zl if chain == 0 else 1 - zl, origin, core)
                if step < (3 if chain == 0 else 2) or (step == 3 and (chain, way) == (0, 0)):
                    to_ring(chain, way, step, piece, piece)
                if chain == 0 and step >= 3:
                    to_pair(piece)
                to_core(piece, piece)

    @pl.when(jnp.logical_not(stays))
    def _():
        row_copy.start()

    @pl.when(stays)
    def _():
        row_keep.start()

    for copy, origin in zip(pair_copies[1:], (y + 5, y + 3, y + 4)):
        copy.wait_recv()
        piece = shard(1 - zl, origin % 8, core)
        to_core(piece, piece)

    def columns_of(k):
        return pl.ds(pl.multiple_of(k * B, B), B)

    def band(at, size):
        return own_rows.at[pl.ds(pl.multiple_of(at, 16), size)]

    keep.wait()
    big_copy.wait()
    for copy in core_copies:
        copy.wait_recv()

    def multiply(k):
        columns = columns_of(k)

        @pl.loop(0, 2)
        def _(half):
            rows = pl.ds(pl.multiple_of(half * 384, 128), 384)
            product = jnp.dot(inverse[rows, :], gathered[:, columns], preferred_element_type=F32)
            part[k, half] = product.reshape(CHUNKS, CHUNK, B)

    def hop(source, target, sends, recvs, chunk, n, device):
        at = chunk * 6 + n
        return send(source, target.at[chunk, n], sends.at[at], recvs.at[at], device)

    far, ahead, behind = (x + 2) % 4, (x + 1) % 4, (x + 3) % 4
    hops = {}

    def x_mid(h):
        hops["x", h, 0] = hop(part.at[far, 0, h], x_in, x_send, x_recv, h, 0, x_device(1))
        hops["x", h, 1] = hop(part.at[far, 1, h], x_in, x_send, x_recv, h, 1, x_device(-1))

    def x_raw_up(h):
        hops["x", h, 2] = hop(part.at[ahead, 1, h], x_in, x_send, x_recv, h, 2, x_device(1))

    def x_raw_down(h):
        hops["x", h, 4] = hop(part.at[behind, 0, h], x_in, x_send, x_recv, h, 4, x_device(-1))

    def x_sum(h):
        hops["x", h, 0].wait_recv()
        part[ahead, 0, h] = part[ahead, 0, h] + x_in[h, 0]
        hops["x", h, 3] = hop(part.at[ahead, 0, h], x_in, x_send, x_recv, h, 3, x_device(1))
        hops["x", h, 1].wait_recv()
        part[behind, 1, h] = part[behind, 1, h] + x_in[h, 1]
        hops["x", h, 5] = hop(part.at[behind, 1, h], x_in, x_send, x_recv, h, 5, x_device(-1))

    z_far, z_ahead, z_behind = (zh + 2) % 4, (zh + 1) % 4, (zh + 3) % 4

    def z_start(h):
        for n in (2, 3, 4, 5):
            hops["x", h, n].wait_recv()
        for way in range(2):
            rows = pl.ds(way * (CHUNK // 2), CHUNK // 2)
            low = part[x, 0, h, rows, :] + x_in[h, 3, rows, :] + x_in[h, 4, rows, :]
            high = part[x, 1, h, rows, :] + x_in[h, 5, rows, :] + x_in[h, 2, rows, :]
            for q in range(4):
                lanes = slice(64 * q, 64 * q + 64)
                z_part[q, h, way] = jnp.concatenate([low[:, lanes], high[:, lanes]], axis=1)
        up, down = z_device(1), z_device(-1)
        hops["z", h, 0] = hop(z_part.at[z_far, h, 0], z_in, z_send, z_recv, h, 0, up)
        hops["z", h, 1] = hop(z_part.at[z_far, h, 1], z_in, z_send, z_recv, h, 1, down)
        hops["z", h, 2] = hop(z_part.at[z_ahead, h, 1], z_in, z_send, z_recv, h, 2, up)
        hops["z", h, 4] = hop(z_part.at[z_behind, h, 0], z_in, z_send, z_recv, h, 4, down)

    def z_sum(h):
        hops["z", h, 0].wait_recv()
        z_part[z_ahead, h, 0] = z_part[z_ahead, h, 0] + z_in[h, 0]
        hops["z", h, 3] = hop(z_part.at[z_ahead, h, 0], z_in, z_send, z_recv, h, 3, z_device(1))
        hops["z", h, 1].wait_recv()
        z_part[z_behind, h, 1] = z_part[z_behind, h, 1] + z_in[h, 1]
        hops["z", h, 5] = hop(z_part.at[z_behind, h, 1], z_in, z_send, z_recv, h, 5, z_device(-1))

    def band_copy(n, at, size, device):
        here = band(at, size)
        return send(here, here, band_send.at[n], band_recv.at[n], device)

    multiply(far)
    x_mid(0)
    multiply(ahead)
    x_raw_up(0)
    multiply(behind)
    x_raw_down(0)
    if CHUNKS > 1:
        x_mid(1)
    multiply(x)

    @pl.when(jnp.logical_not(stays))
    def _():
        row_copy.wait_recv()

    @pl.when(stays)
    def _():
        row_keep.wait()

    slices = [
        send(
            row_in.at[:, columns_of((x + i) % 4)],
            band(share * ROWS, ROWS),
            slice_send.at[i - 1],
            slice_recv.at[i - 1],
            x_device(i),
        )
        for i in (1, 3, 2)
    ]
    slice_keep = pltpu.make_async_copy(
        row_in.at[:, columns_of(x)], band(share * ROWS, ROWS), local_sem.at[3]
    )
    slice_keep.start()
    for h in range(CHUNKS):
        x_sum(h)
        if h + 1 < CHUNKS:
            x_raw_up(h + 1)
            x_raw_down(h + 1)
        if h + 2 < CHUNKS:
            x_mid(h + 2)
        if h == 0:
            slice_keep.wait()
            for copy in slices:
                copy.wait_recv()
            band_up = band_copy(0, zh * 192, 192, z_device(1))
            band_down = band_copy(1, zh * 192, 192, z_device(-1))
        if h == 1:
            band_up.wait_recv()
            far_up = band_copy(2, z_behind * 192, 96, z_device(1))
            band_down.wait_recv()
            far_down = band_copy(3, z_ahead * 192 + 96, 96, z_device(-1))
        if h >= 2:
            z_sum(h - 2)
        if h >= 1:
            z_start(h - 1)
    if CHUNKS > 1:
        z_sum(CHUNKS - 2)
    z_start(CHUNKS - 1)
    z_sum(CHUNKS - 1)
    far_up.wait_recv()
    far_down.wait_recv()

    half_rows = CHUNK // 2
    lane = lax.broadcasted_iota(jnp.int32, (half_rows, 128), 1)
    row = lax.broadcasted_iota(jnp.int32, (half_rows, 128), 0) + jnp.where(lane < 64, 0, 384)
    kept = [-listed(c * 3 + i) for i in range(3)]
    level = lax.broadcasted_iota(jnp.int32, (NK, 1), 0) == x
    kept = [jnp.sum(jnp.where(level, k, 0.0), axis=0, keepdims=True) for k in kept]
    left_sum = jnp.zeros((B, 128), F32)
    right_sum = jnp.zeros((B, 128), F32)
    over_rows = (((0,), (0,)), ((), ()))
    for h in range(CHUNKS):
        for n in (2, 3, 4, 5):
            hops["z", h, n].wait_recv()
        for way in range(2):
            start = h * CHUNK + way * half_rows
            at = row + start
            keep_row = jnp.where(at < B, kept[0], jnp.where(at < 2 * B, kept[1], kept[2]))
            first, second = (3, 4) if way == 0 else (5, 2)
            total = (z_part[zh, h, way] + z_in[h, first] + z_in[h, second]) * keep_row
            off_out[pl.ds(start, half_rows), :] = total[:, :64].astype(BF16)
            off_out[pl.ds(384 + start, half_rows), :] = total[:, 64:].astype(BF16)
            big = total.astype(BF16)
            small = (total - big.astype(F32)).astype(BF16)
            left = own_rows[pl.ds(start, half_rows), :]
            right = own_rows[pl.ds(384 + start, half_rows), :]
            for piece in (big, small):
                left_sum = left_sum + lax.dot_general(
                    left, piece, over_rows, preferred_element_type=F32
                )
                right_sum = right_sum + lax.dot_general(
                    right, piece, over_rows, preferred_element_type=F32
                )
    lane = lax.broadcasted_iota(jnp.int32, (B, 128), 1)
    term = jnp.where(lane < 64, left_sum, right_sum).reshape(2, 8, 2, 8, 128)

    for q in range(2):
        core_part[q] = term[:, :, q]
    copy = send(
        core_part.at[1 - core], core_in, sum_sem.at[0], sum_sem.at[1], col_device(zl, y, 1 - core)
    )
    copy.wait_recv()
    y_part[...] = core_part[core] + core_in[...]
    y_copies = []
    for n in range(1, 16):
        z_to, y_to = (zl + n // 8) % 2, (y + n) % 8
        y_copies.append(
            send(
                y_part.at[z_to, y_to],
                y_in.at[n - 1],
                y_send.at[n - 1],
                y_recv.at[n - 1],
                col_device(z_to, y_to, core),
            )
        )
    pivot_copy.wait()
    total = y_part[zl, y]
    for n, copy in enumerate(y_copies):
        copy.wait_recv()
        total = total + y_in[n]
    diag_out[...] = pivot[...] - (total[:, :64] + total[:, 64:])

    for copy in sent:
        copy.wait_send()

    @pl.when(jnp.logical_not(stays))
    def _():
        row_copy.wait_send()


def body(ancestor_inverse, lower_panel, pivot_inverse, struct_list):
    vmem = pl.BlockSpec(memory_space=pltpu.VMEM)
    hbm = pl.BlockSpec(memory_space=pltpu.HBM)
    dma = pltpu.SemaphoreType.DMA
    hop_sems = [dma((6 * CHUNKS,))] * 4
    return pl.pallas_call(
        kernel,
        out_shape=(
            jax.ShapeDtypeStruct((768, 64), BF16),
            jax.ShapeDtypeStruct((8, 64), F32),
        ),
        in_specs=[vmem, hbm, hbm, hbm],
        out_specs=(vmem, vmem),
        scratch_shapes=[
            pltpu.VMEM((768, 1536), BF16),
            pltpu.VMEM((8, 64), F32),
            pltpu.VMEM((ROWS, 1024), BF16),
            pltpu.VMEM((ROWS, 1024), BF16),
            pltpu.VMEM((1536, 1024), BF16),
            pltpu.VMEM((ROWS, 1024), BF16),
            pltpu.VMEM((768, B), BF16),
            pltpu.VMEM((4, 2, CHUNKS, CHUNK, B), F32),
            pltpu.VMEM((CHUNKS, 6, CHUNK, B), F32),
            pltpu.VMEM((4, CHUNKS, 2, CHUNK // 2, 128), F32),
            pltpu.VMEM((CHUNKS, 6, CHUNK // 2, 128), F32),
            pltpu.VMEM((2, 2, 8, 8, 128), F32),
            pltpu.VMEM((2, 8, 8, 128), F32),
            pltpu.VMEM((2, 8, 8, 128), F32),
            pltpu.VMEM((15, 8, 128), F32),
            dma((5,)),
            dma((8,)),
            dma((16,)),
            dma((16,)),
            dma((16,)),
            dma((16,)),
            dma((3,)),
            dma((3,)),
            dma((3,)),
            dma((4,)),
            dma((4,)),
            *hop_sems,
            dma((2,)),
            dma((15,)),
            dma((15,)),
        ],
        compiler_params=pltpu.CompilerParams(
            collective_id=0, has_side_effects=True
        ),
    )(struct_list, ancestor_inverse, lower_panel, pivot_inverse)


def solution(mesh):
    placed = (P("pcol", "prow"), P(("prow", "pcol"), None), P("pcol", "prow"), P())
    return jax.shard_map(
        body,
        mesh=mesh,
        in_specs=placed,
        out_specs=(P("pcol", "prow"), P("pcol", "prow")),
        check_vma=False,
    )
```

```python
import jax
import jax.numpy as jnp
from jax import lax
from jax.experimental import pallas as pl
from jax.experimental.pallas import tpu as pltpu
from jax.sharding import PartitionSpec as P

B = 256
NK = 4
MESH = pl.DeviceIdType.MESH
F32 = jnp.float32
BF16 = jnp.bfloat16
ROWS = 48
SHARES = 16
CHUNKS = 2
CHUNK = 384 // CHUNKS


def remote(src, dst, send, recv, device):
    return pltpu.make_async_remote_copy(
        src_ref=src, dst_ref=dst, send_sem=send, recv_sem=recv, device_id=device, device_id_type=MESH
    )


def kernel(
    lists,
    inverse_hbm,
    lower_hbm,
    pivot_hbm,
    off_out,
    diag_out,
    inverse,
    pivot,
    raw,
    lower,
    gathered,
    row_in,
    own_rows,
    part,
    x_in,
    z_part,
    z_in,
    core_part,
    core_in,
    y_part,
    y_in,
    local_sem,
    pair_sem,
    ring_send,
    ring_recv,
    core_send,
    core_recv,
    row_sem,
    slice_send,
    slice_recv,
    band_send,
    band_recv,
    x_send,
    x_recv,
    z_send,
    z_recv,
    sum_sem,
    y_send,
    y_recv,
):
    r, c = lax.axis_index("prow"), lax.axis_index("pcol")
    x, zh = r // 4, r % 4
    zl, y, core = c // 16, (c % 16) // 2, c % 2
    share = zh * 4 + x
    source = {"prow": c // 2, "pcol": (c % 2) * SHARES + share}
    target_row, target_col = (c % 4) * 4 + (c % SHARES) // 4, 2 * r + c // SHARES
    stays = (target_row == r) & (target_col == c)

    def col_device(z_lo, y_at, core_at):
        return {"prow": r, "pcol": z_lo * 16 + (y_at % 8) * 2 + core_at}

    def x_device(step):
        return {"prow": ((x + step + 4) % 4) * 4 + zh, "pcol": c}

    def z_device(step):
        return {"prow": x * 4 + (zh + step + 4) % 4, "pcol": c}

    big_copy = pltpu.make_async_copy(inverse_hbm, inverse, local_sem.at[1])
    big_copy.start()
    pivot_copy = pltpu.make_async_copy(pivot_hbm, pivot, local_sem.at[2])
    pivot_copy.start()

    raw_copy = pltpu.make_async_copy(lower_hbm, raw, local_sem.at[4])
    raw_copy.start()

    barrier = pltpu.get_barrier_semaphore()
    friends = [col_device(zl, y + i, core) for i in range(1, 8)]
    friends += [col_device(1 - zl, y + i, core) for i in range(8)] + [col_device(zl, y, 1 - core)]
    friends += [x_device(1), x_device(2), x_device(3), z_device(1), z_device(-1)]
    for device in friends:
        pl.semaphore_signal(barrier, inc=1, device_id=device, device_id_type=MESH)

    @pl.when(jnp.logical_not(stays))
    def _():
        pl.semaphore_signal(barrier, inc=1, device_id=source, device_id_type=MESH)

    def listed(ancestor):
        found = jnp.where(lists[...] == ancestor, 1.0, 0.0)
        return jnp.max(found, axis=1, keepdims=True)

    raw_copy.wait()
    begin = (r * 32 + c) * ROWS
    first = begin // B
    in_first = lax.broadcasted_iota(jnp.int32, (ROWS, B), 0) + begin < (first + 1) * B
    of_first, of_next = listed(first), listed(first + 1)
    for k in range(NK):
        columns = pl.ds(k * B, B)
        member = jnp.where(in_first, of_first[k : k + 1, :], of_next[k : k + 1, :])
        lower[:, columns] = (raw[:, columns].astype(F32) * member).astype(BF16)

    pl.semaphore_wait(barrier, len(friends) + 1 - stays.astype(jnp.int32))

    def shard(z_lo, y_at, core_at):
        at = (z_lo * 16 + y_at * 2 + core_at) * ROWS
        return gathered.at[pl.ds(pl.multiple_of(at, 16), ROWS)]

    sent = []
    core_copies = []

    def send(src, dst, send_sem, recv_sem, device):
        copy = remote(src, dst, send_sem, recv_sem, device)
        copy.start()
        sent.append(copy)
        return copy

    def to_core(src, dst):
        n = len(core_copies)
        core_copies.append(
            send(src, dst, core_send.at[n], core_recv.at[n], col_device(zl, y, 1 - core))
        )

    ring = {}

    def to_ring(chain, way, step, src, dst):
        n = (chain * 2 + way) * 4 + step
        device = col_device(zl, y + (1 if way == 0 else 7), core)
        ring[chain, way, step] = send(src, dst, ring_send.at[n], ring_recv.at[n], device)

    mine = shard(zl, y, core)
    pair = send(lower, mine, pair_sem.at[0], pair_sem.at[1], col_device(1 - zl, y, core))
    to_ring(0, 0, 0, lower, mine)
    to_ring(0, 1, 0, lower, mine)
    to_core(lower, mine)
    keep = pltpu.make_async_copy(lower, mine, local_sem.at[0])
    keep.start()
    row_copy = remote(
        lower, row_in, row_sem.at[0], row_sem.at[1], {"prow": target_row, "pcol": target_col}
    )
    row_keep = pltpu.make_async_copy(lower, row_in, row_sem.at[2])

    pair.wait_recv()
    theirs = shard(1 - zl, y, core)
    to_ring(1, 0, 0, theirs, theirs)
    to_ring(1, 1, 0, theirs, theirs)
    to_core(theirs, theirs)
    @pl.when(jnp.logical_not(stays))
    def _():
        row_copy.start()

    @pl.when(stays)
    def _():
        row_keep.start()

    for step in range(1, 5):
        for chain in range(2):
            for way in range(2):
                if (chain, way, step - 1) not in ring:
                    continue
                ring[chain, way, step - 1].wait_recv()
                origin = (y + (8 - step if way == 0 else step)) % 8
                piece = shard(zl if chain == 0 else 1 - zl, origin, core)
                if step < 3 or (step == 3 and chain == way):
                    to_ring(chain, way, step, piece, piece)
                to_core(piece, piece)

    def columns_of(k):
        return pl.ds(pl.multiple_of(k * B, B), B)

    def band(at, size):
        return own_rows.at[pl.ds(pl.multiple_of(at, 16), size)]

    keep.wait()
    big_copy.wait()
    for copy in core_copies:
        copy.wait_recv()

    def multiply(k):
        columns = columns_of(k)

        @pl.loop(0, 2)
        def _(half):
            rows = pl.ds(pl.multiple_of(half * 384, 128), 384)
            product = jnp.dot(inverse[rows, :], gathered[:, columns], preferred_element_type=F32)
            part[k, half] = product.reshape(CHUNKS, CHUNK, B)

    def hop(source, target, sends, recvs, chunk, n, device):
        at = chunk * 6 + n
        return send(source, target.at[chunk, n], sends.at[at], recvs.at[at], device)

    far, ahead, behind = (x + 2) % 4, (x + 1) % 4, (x + 3) % 4
    hops = {}

    def x_mid(h):
        hops["x", h, 0] = hop(part.at[far, 0, h], x_in, x_send, x_recv, h, 0, x_device(1))
        hops["x", h, 1] = hop(part.at[far, 1, h], x_in, x_send, x_recv, h, 1, x_device(-1))

    def x_raw_up(h):
        hops["x", h, 2] = hop(part.at[ahead, 1, h], x_in, x_send, x_recv, h, 2, x_device(1))

    def x_raw_down(h):
        hops["x", h, 4] = hop(part.at[behind, 0, h], x_in, x_send, x_recv, h, 4, x_device(-1))

    def x_sum(h):
        hops["x", h, 0].wait_recv()
        part[ahead, 0, h] = part[ahead, 0, h] + x_in[h, 0]
        hops["x", h, 3] = hop(part.at[ahead, 0, h], x_in, x_send, x_recv, h, 3, x_device(1))
        hops["x", h, 1].wait_recv()
        part[behind, 1, h] = part[behind, 1, h] + x_in[h, 1]
        hops["x", h, 5] = hop(part.at[behind, 1, h], x_in, x_send, x_recv, h, 5, x_device(-1))

    z_far, z_ahead, z_behind = (zh + 2) % 4, (zh + 1) % 4, (zh + 3) % 4

    def z_start(h):
        for n in (2, 3, 4, 5):
            hops["x", h, n].wait_recv()
        for way in range(2):
            rows = pl.ds(way * (CHUNK // 2), CHUNK // 2)
            low = part[x, 0, h, rows, :] + x_in[h, 3, rows, :] + x_in[h, 4, rows, :]
            high = part[x, 1, h, rows, :] + x_in[h, 5, rows, :] + x_in[h, 2, rows, :]
            for q in range(4):
                lanes = slice(64 * q, 64 * q + 64)
                z_part[q, h, way] = jnp.concatenate([low[:, lanes], high[:, lanes]], axis=1)
        up, down = z_device(1), z_device(-1)
        hops["z", h, 0] = hop(z_part.at[z_far, h, 0], z_in, z_send, z_recv, h, 0, up)
        hops["z", h, 1] = hop(z_part.at[z_far, h, 1], z_in, z_send, z_recv, h, 1, down)
        hops["z", h, 2] = hop(z_part.at[z_ahead, h, 1], z_in, z_send, z_recv, h, 2, up)
        hops["z", h, 4] = hop(z_part.at[z_behind, h, 0], z_in, z_send, z_recv, h, 4, down)

    def z_sum(h):
        hops["z", h, 0].wait_recv()
        z_part[z_ahead, h, 0] = z_part[z_ahead, h, 0] + z_in[h, 0]
        hops["z", h, 3] = hop(z_part.at[z_ahead, h, 0], z_in, z_send, z_recv, h, 3, z_device(1))
        hops["z", h, 1].wait_recv()
        z_part[z_behind, h, 1] = z_part[z_behind, h, 1] + z_in[h, 1]
        hops["z", h, 5] = hop(z_part.at[z_behind, h, 1], z_in, z_send, z_recv, h, 5, z_device(-1))

    def band_copy(n, at, size, device):
        here = band(at, size)
        return send(here, here, band_send.at[n], band_recv.at[n], device)

    multiply(far)
    x_mid(0)
    multiply(ahead)
    x_raw_up(0)
    multiply(behind)
    x_raw_down(0)
    if CHUNKS > 1:
        x_mid(1)
    multiply(x)

    @pl.when(jnp.logical_not(stays))
    def _():
        row_copy.wait_recv()

    @pl.when(stays)
    def _():
        row_keep.wait()

    slices = [
        send(
            row_in.at[:, columns_of((x + i) % 4)],
            band(share * ROWS, ROWS),
            slice_send.at[i - 1],
            slice_recv.at[i - 1],
            x_device(i),
        )
        for i in (1, 3, 2)
    ]
    slice_keep = pltpu.make_async_copy(
        row_in.at[:, columns_of(x)], band(share * ROWS, ROWS), local_sem.at[3]
    )
    slice_keep.start()
    for h in range(CHUNKS):
        x_sum(h)
        if h + 1 < CHUNKS:
            x_raw_up(h + 1)
            x_raw_down(h + 1)
        if h + 2 < CHUNKS:
            x_mid(h + 2)
        if h == 0:
            slice_keep.wait()
            for copy in slices:
                copy.wait_recv()
            band_up = band_copy(0, zh * 192, 192, z_device(1))
            band_down = band_copy(1, zh * 192, 192, z_device(-1))
        if h == 1:
            band_up.wait_recv()
            far_up = band_copy(2, z_behind * 192, 96, z_device(1))
            band_down.wait_recv()
            far_down = band_copy(3, z_ahead * 192 + 96, 96, z_device(-1))
        if h >= 2:
            z_sum(h - 2)
        if h >= 1:
            z_start(h - 1)
    if CHUNKS > 1:
        z_sum(CHUNKS - 2)
    z_start(CHUNKS - 1)
    z_sum(CHUNKS - 1)
    far_up.wait_recv()
    far_down.wait_recv()

    half_rows = CHUNK // 2
    lane = lax.broadcasted_iota(jnp.int32, (half_rows, 128), 1)
    row = lax.broadcasted_iota(jnp.int32, (half_rows, 128), 0) + jnp.where(lane < 64, 0, 384)
    kept = [-listed(c * 3 + i) for i in range(3)]
    level = lax.broadcasted_iota(jnp.int32, (NK, 1), 0) == x
    kept = [jnp.sum(jnp.where(level, k, 0.0), axis=0, keepdims=True) for k in kept]
    left_sum = jnp.zeros((B, 128), F32)
    right_sum = jnp.zeros((B, 128), F32)
    over_rows = (((0,), (0,)), ((), ()))
    for h in range(CHUNKS):
        for n in (2, 3, 4, 5):
            hops["z", h, n].wait_recv()
        for way in range(2):
            start = h * CHUNK + way * half_rows
            at = row + start
            keep_row = jnp.where(at < B, kept[0], jnp.where(at < 2 * B, kept[1], kept[2]))
            first, second = (3, 4) if way == 0 else (5, 2)
            total = (z_part[zh, h, way] + z_in[h, first] + z_in[h, second]) * keep_row
            off_out[pl.ds(start, half_rows), :] = total[:, :64].astype(BF16)
            off_out[pl.ds(384 + start, half_rows), :] = total[:, 64:].astype(BF16)
            big = total.astype(BF16)
            small = (total - big.astype(F32)).astype(BF16)
            left = own_rows[pl.ds(start, half_rows), :]
            right = own_rows[pl.ds(384 + start, half_rows), :]
            for piece in (big, small):
                left_sum = left_sum + lax.dot_general(
                    left, piece, over_rows, preferred_element_type=F32
                )
                right_sum = right_sum + lax.dot_general(
                    right, piece, over_rows, preferred_element_type=F32
                )
    lane = lax.broadcasted_iota(jnp.int32, (B, 128), 1)
    term = jnp.where(lane < 64, left_sum, right_sum).reshape(2, 8, 2, 8, 128)

    for q in range(2):
        core_part[q] = term[:, :, q]
    copy = send(
        core_part.at[1 - core], core_in, sum_sem.at[0], sum_sem.at[1], col_device(zl, y, 1 - core)
    )
    copy.wait_recv()
    y_part[...] = core_part[core] + core_in[...]
    y_copies = []
    for n in range(1, 16):
        z_to, y_to = (zl + n // 8) % 2, (y + n) % 8
        y_copies.append(
            send(
                y_part.at[z_to, y_to],
                y_in.at[n - 1],
                y_send.at[n - 1],
                y_recv.at[n - 1],
                col_device(z_to, y_to, core),
            )
        )
    pivot_copy.wait()
    total = y_part[zl, y]
    for n, copy in enumerate(y_copies):
        copy.wait_recv()
        total = total + y_in[n]
    diag_out[...] = pivot[...] - (total[:, :64] + total[:, 64:])

    for copy in sent:
        copy.wait_send()

    @pl.when(jnp.logical_not(stays))
    def _():
        row_copy.wait_send()


def body(ancestor_inverse, lower_panel, pivot_inverse, struct_list):
    vmem = pl.BlockSpec(memory_space=pltpu.VMEM)
    hbm = pl.BlockSpec(memory_space=pltpu.HBM)
    dma = pltpu.SemaphoreType.DMA
    hop_sems = [dma((6 * CHUNKS,))] * 4
    return pl.pallas_call(
        kernel,
        out_shape=(
            jax.ShapeDtypeStruct((768, 64), BF16),
            jax.ShapeDtypeStruct((8, 64), F32),
        ),
        in_specs=[vmem, hbm, hbm, hbm],
        out_specs=(vmem, vmem),
        scratch_shapes=[
            pltpu.VMEM((768, 1536), BF16),
            pltpu.VMEM((8, 64), F32),
            pltpu.VMEM((ROWS, 1024), BF16),
            pltpu.VMEM((ROWS, 1024), BF16),
            pltpu.VMEM((1536, 1024), BF16),
            pltpu.VMEM((ROWS, 1024), BF16),
            pltpu.VMEM((768, B), BF16),
            pltpu.VMEM((4, 2, CHUNKS, CHUNK, B), F32),
            pltpu.VMEM((CHUNKS, 6, CHUNK, B), F32),
            pltpu.VMEM((4, CHUNKS, 2, CHUNK // 2, 128), F32),
            pltpu.VMEM((CHUNKS, 6, CHUNK // 2, 128), F32),
            pltpu.VMEM((2, 2, 8, 8, 128), F32),
            pltpu.VMEM((2, 8, 8, 128), F32),
            pltpu.VMEM((2, 8, 8, 128), F32),
            pltpu.VMEM((15, 8, 128), F32),
            dma((5,)),
            dma((2,)),
            dma((16,)),
            dma((16,)),
            dma((16,)),
            dma((16,)),
            dma((3,)),
            dma((3,)),
            dma((3,)),
            dma((4,)),
            dma((4,)),
            *hop_sems,
            dma((2,)),
            dma((15,)),
            dma((15,)),
        ],
        compiler_params=pltpu.CompilerParams(
            collective_id=0, has_side_effects=True
        ),
    )(struct_list, ancestor_inverse, lower_panel, pivot_inverse)


def solution(mesh):
    placed = (P("pcol", "prow"), P(("prow", "pcol"), None), P("pcol", "prow"), P())
    return jax.shard_map(
        body,
        mesh=mesh,
        in_specs=placed,
        out_specs=(P("pcol", "prow"), P("pcol", "prow")),
        check_vma=False,
    )
```

```python
import jax
import jax.numpy as jnp
from jax import lax
from jax.experimental import pallas as pl
from jax.experimental.pallas import tpu as pltpu
from jax.sharding import PartitionSpec as P

B = 256
NK = 4
MESH = pl.DeviceIdType.MESH
F32 = jnp.float32
BF16 = jnp.bfloat16
ROWS = 48
SHARES = 16
CHUNKS = 2
CHUNK = 384 // CHUNKS


def remote(src, dst, send, recv, device):
    return pltpu.make_async_remote_copy(
        src_ref=src, dst_ref=dst, send_sem=send, recv_sem=recv, device_id=device, device_id_type=MESH
    )


def kernel(
    lists,
    inverse_hbm,
    lower_hbm,
    pivot_hbm,
    off_out,
    diag_out,
    inverse,
    pivot,
    raw,
    lower,
    gathered,
    row_in,
    own_rows,
    part,
    x_in,
    z_part,
    z_in,
    core_part,
    core_in,
    y_part,
    y_in,
    local_sem,
    pair_sem,
    ring_send,
    ring_recv,
    core_send,
    core_recv,
    row_sem,
    slice_send,
    slice_recv,
    band_send,
    band_recv,
    x_send,
    x_recv,
    z_send,
    z_recv,
    sum_sem,
    y_send,
    y_recv,
):
    r, c = lax.axis_index("prow"), lax.axis_index("pcol")
    x, zh = r // 4, r % 4
    zl, y, core = c // 16, (c % 16) // 2, c % 2
    share = zh * 4 + x
    source = {"prow": c // 2, "pcol": (c % 2) * SHARES + share}
    target_row, target_col = (c % 4) * 4 + (c % SHARES) // 4, 2 * r + c // SHARES
    stays = (target_row == r) & (target_col == c)

    def col_device(z_lo, y_at, core_at):
        return {"prow": r, "pcol": z_lo * 16 + (y_at % 8) * 2 + core_at}

    def x_device(step):
        return {"prow": ((x + step + 4) % 4) * 4 + zh, "pcol": c}

    def z_device(step):
        return {"prow": x * 4 + (zh + step + 4) % 4, "pcol": c}

    big_copy = pltpu.make_async_copy(inverse_hbm, inverse, local_sem.at[1])
    big_copy.start()
    pivot_copy = pltpu.make_async_copy(pivot_hbm, pivot, local_sem.at[2])
    pivot_copy.start()

    raw_copy = pltpu.make_async_copy(lower_hbm, raw, local_sem.at[4])
    raw_copy.start()

    barrier = pltpu.get_barrier_semaphore()
    friends = [col_device(zl, y + i, core) for i in range(1, 8)]
    friends += [col_device(1 - zl, y + i, core) for i in range(8)] + [col_device(zl, y, 1 - core)]
    friends += [x_device(1), x_device(2), x_device(3), z_device(1), z_device(-1)]
    for device in friends:
        pl.semaphore_signal(barrier, inc=1, device_id=device, device_id_type=MESH)

    @pl.when(jnp.logical_not(stays))
    def _():
        pl.semaphore_signal(barrier, inc=1, device_id=source, device_id_type=MESH)

    def listed(ancestor):
        found = jnp.where(lists[...] == ancestor, 1.0, 0.0)
        return jnp.max(found, axis=1, keepdims=True)

    raw_copy.wait()
    begin = (r * 32 + c) * ROWS
    first = begin // B
    in_first = lax.broadcasted_iota(jnp.int32, (ROWS, B), 0) + begin < (first + 1) * B
    of_first, of_next = listed(first), listed(first + 1)
    for k in range(NK):
        columns = pl.ds(k * B, B)
        member = jnp.where(in_first, of_first[k : k + 1, :], of_next[k : k + 1, :])
        lower[:, columns] = (raw[:, columns].astype(F32) * member).astype(BF16)

    pl.semaphore_wait(barrier, len(friends) + 1 - stays.astype(jnp.int32))

    def shard(z_lo, y_at, core_at):
        at = (z_lo * 16 + y_at * 2 + core_at) * ROWS
        return gathered.at[pl.ds(pl.multiple_of(at, 16), ROWS)]

    sent = []
    core_copies = []

    def send(src, dst, send_sem, recv_sem, device):
        copy = remote(src, dst, send_sem, recv_sem, device)
        copy.start()
        sent.append(copy)
        return copy

    def to_core(src, dst):
        n = len(core_copies)
        core_copies.append(
            send(src, dst, core_send.at[n], core_recv.at[n], col_device(zl, y, 1 - core))
        )

    ring = {}

    def to_ring(chain, way, step, src, dst):
        n = (chain * 2 + way) * 4 + step
        device = col_device(zl, y + (1 if way == 0 else 7), core)
        ring[chain, way, step] = send(src, dst, ring_send.at[n], ring_recv.at[n], device)

    mine = shard(zl, y, core)
    pair = send(lower, mine, pair_sem.at[0], pair_sem.at[1], col_device(1 - zl, y, core))
    to_ring(0, 0, 0, lower, mine)
    to_ring(0, 1, 0, lower, mine)
    to_core(lower, mine)
    keep = pltpu.make_async_copy(lower, mine, local_sem.at[0])
    keep.start()
    row_copy = remote(
        lower, row_in, row_sem.at[0], row_sem.at[1], {"prow": target_row, "pcol": target_col}
    )
    row_keep = pltpu.make_async_copy(lower, row_in, row_sem.at[2])

    pair.wait_recv()
    theirs = shard(1 - zl, y, core)
    to_ring(1, 0, 0, theirs, theirs)
    to_ring(1, 1, 0, theirs, theirs)
    to_core(theirs, theirs)
    for step in range(1, 5):
        for chain in range(2):
            for way in range(2):
                if (chain, way, step - 1) not in ring:
                    continue
                ring[chain, way, step - 1].wait_recv()
                origin = (y + (8 - step if way == 0 else step)) % 8
                piece = shard(zl if chain == 0 else 1 - zl, origin, core)
                if step < 3 or (step == 3 and chain == way):
                    to_ring(chain, way, step, piece, piece)
                to_core(piece, piece)

    @pl.when(jnp.logical_not(stays))
    def _():
        row_copy.start()

    @pl.when(stays)
    def _():
        row_keep.start()

    def columns_of(k):
        return pl.ds(pl.multiple_of(k * B, B), B)

    def band(at, size):
        return own_rows.at[pl.ds(pl.multiple_of(at, 16), size)]

    keep.wait()
    big_copy.wait()
    for copy in core_copies:
        copy.wait_recv()

    def multiply(k):
        columns = columns_of(k)

        @pl.loop(0, 2)
        def _(half):
            rows = pl.ds(pl.multiple_of(half * 384, 128), 384)
            product = jnp.dot(inverse[rows, :], gathered[:, columns], preferred_element_type=F32)
            part[k, half] = product.reshape(CHUNKS, CHUNK, B)

    def hop(source, target, sends, recvs, chunk, n, device):
        at = chunk * 6 + n
        return send(source, target.at[chunk, n], sends.at[at], recvs.at[at], device)

    far, ahead, behind = (x + 2) % 4, (x + 1) % 4, (x + 3) % 4
    hops = {}

    def x_mid(h):
        hops["x", h, 0] = hop(part.at[far, 0, h], x_in, x_send, x_recv, h, 0, x_device(1))
        hops["x", h, 1] = hop(part.at[far, 1, h], x_in, x_send, x_recv, h, 1, x_device(-1))

    def x_raw_up(h):
        hops["x", h, 2] = hop(part.at[ahead, 1, h], x_in, x_send, x_recv, h, 2, x_device(1))

    def x_raw_down(h):
        hops["x", h, 4] = hop(part.at[behind, 0, h], x_in, x_send, x_recv, h, 4, x_device(-1))

    def x_sum(h):
        hops["x", h, 0].wait_recv()
        part[ahead, 0, h] = part[ahead, 0, h] + x_in[h, 0]
        hops["x", h, 3] = hop(part.at[ahead, 0, h], x_in, x_send, x_recv, h, 3, x_device(1))
        hops["x", h, 1].wait_recv()
        part[behind, 1, h] = part[behind, 1, h] + x_in[h, 1]
        hops["x", h, 5] = hop(part.at[behind, 1, h], x_in, x_send, x_recv, h, 5, x_device(-1))

    z_far, z_ahead, z_behind = (zh + 2) % 4, (zh + 1) % 4, (zh + 3) % 4

    def z_start(h):
        for n in (2, 3, 4, 5):
            hops["x", h, n].wait_recv()
        for way in range(2):
            rows = pl.ds(way * (CHUNK // 2), CHUNK // 2)
            low = part[x, 0, h, rows, :] + x_in[h, 3, rows, :] + x_in[h, 4, rows, :]
            high = part[x, 1, h, rows, :] + x_in[h, 5, rows, :] + x_in[h, 2, rows, :]
            for q in range(4):
                lanes = slice(64 * q, 64 * q + 64)
                z_part[q, h, way] = jnp.concatenate([low[:, lanes], high[:, lanes]], axis=1)
        up, down = z_device(1), z_device(-1)
        hops["z", h, 0] = hop(z_part.at[z_far, h, 0], z_in, z_send, z_recv, h, 0, up)
        hops["z", h, 1] = hop(z_part.at[z_far, h, 1], z_in, z_send, z_recv, h, 1, down)
        hops["z", h, 2] = hop(z_part.at[z_ahead, h, 1], z_in, z_send, z_recv, h, 2, up)
        hops["z", h, 4] = hop(z_part.at[z_behind, h, 0], z_in, z_send, z_recv, h, 4, down)

    def z_sum(h):
        hops["z", h, 0].wait_recv()
        z_part[z_ahead, h, 0] = z_part[z_ahead, h, 0] + z_in[h, 0]
        hops["z", h, 3] = hop(z_part.at[z_ahead, h, 0], z_in, z_send, z_recv, h, 3, z_device(1))
        hops["z", h, 1].wait_recv()
        z_part[z_behind, h, 1] = z_part[z_behind, h, 1] + z_in[h, 1]
        hops["z", h, 5] = hop(z_part.at[z_behind, h, 1], z_in, z_send, z_recv, h, 5, z_device(-1))

    def band_copy(n, at, size, device):
        here = band(at, size)
        return send(here, here, band_send.at[n], band_recv.at[n], device)

    multiply(far)
    x_mid(0)
    multiply(ahead)
    x_raw_up(0)
    multiply(behind)
    x_raw_down(0)
    if CHUNKS > 1:
        x_mid(1)
    multiply(x)

    x_sum(0)
    x_raw_up(1)
    x_raw_down(1)
    x_sum(1)
    z_start(0)

    @pl.when(jnp.logical_not(stays))
    def _():
        row_copy.wait_recv()

    @pl.when(stays)
    def _():
        row_keep.wait()

    slices = [
        send(
            row_in.at[:, columns_of((x + i) % 4)],
            band(share * ROWS, ROWS),
            slice_send.at[i - 1],
            slice_recv.at[i - 1],
            x_device(i),
        )
        for i in (1, 3, 2)
    ]
    slice_keep = pltpu.make_async_copy(
        row_in.at[:, columns_of(x)], band(share * ROWS, ROWS), local_sem.at[3]
    )
    slice_keep.start()
    z_sum(0)
    slice_keep.wait()
    for copy in slices:
        copy.wait_recv()
    band_up = band_copy(0, zh * 192, 192, z_device(1))
    band_down = band_copy(1, zh * 192, 192, z_device(-1))
    z_start(1)
    z_sum(1)
    band_up.wait_recv()
    far_up = band_copy(2, z_behind * 192, 96, z_device(1))
    band_down.wait_recv()
    far_down = band_copy(3, z_ahead * 192 + 96, 96, z_device(-1))
    far_up.wait_recv()
    far_down.wait_recv()

    half_rows = CHUNK // 2
    lane = lax.broadcasted_iota(jnp.int32, (half_rows, 128), 1)
    row = lax.broadcasted_iota(jnp.int32, (half_rows, 128), 0) + jnp.where(lane < 64, 0, 384)
    kept = [-listed(c * 3 + i) for i in range(3)]
    level = lax.broadcasted_iota(jnp.int32, (NK, 1), 0) == x
    kept = [jnp.sum(jnp.where(level, k, 0.0), axis=0, keepdims=True) for k in kept]
    left_sum = jnp.zeros((B, 128), F32)
    right_sum = jnp.zeros((B, 128), F32)
    over_rows = (((0,), (0,)), ((), ()))
    for h in range(CHUNKS):
        for n in (2, 3, 4, 5):
            hops["z", h, n].wait_recv()
        for way in range(2):
            start = h * CHUNK + way * half_rows
            at = row + start
            keep_row = jnp.where(at < B, kept[0], jnp.where(at < 2 * B, kept[1], kept[2]))
            first, second = (3, 4) if way == 0 else (5, 2)
            total = (z_part[zh, h, way] + z_in[h, first] + z_in[h, second]) * keep_row
            off_out[pl.ds(start, half_rows), :] = total[:, :64].astype(BF16)
            off_out[pl.ds(384 + start, half_rows), :] = total[:, 64:].astype(BF16)
            big = total.astype(BF16)
            small = (total - big.astype(F32)).astype(BF16)
            left = own_rows[pl.ds(start, half_rows), :]
            right = own_rows[pl.ds(384 + start, half_rows), :]
            for piece in (big, small):
                left_sum = left_sum + lax.dot_general(
                    left, piece, over_rows, preferred_element_type=F32
                )
                right_sum = right_sum + lax.dot_general(
                    right, piece, over_rows, preferred_element_type=F32
                )
    lane = lax.broadcasted_iota(jnp.int32, (B, 128), 1)
    term = jnp.where(lane < 64, left_sum, right_sum).reshape(2, 8, 2, 8, 128)

    for q in range(2):
        core_part[q] = term[:, :, q]
    copy = send(
        core_part.at[1 - core], core_in, sum_sem.at[0], sum_sem.at[1], col_device(zl, y, 1 - core)
    )
    copy.wait_recv()
    y_part[...] = core_part[core] + core_in[...]
    y_copies = []
    for n in range(1, 16):
        z_to, y_to = (zl + n // 8) % 2, (y + n) % 8
        y_copies.append(
            send(
                y_part.at[z_to, y_to],
                y_in.at[n - 1],
                y_send.at[n - 1],
                y_recv.at[n - 1],
                col_device(z_to, y_to, core),
            )
        )
    pivot_copy.wait()
    total = y_part[zl, y]
    for n, copy in enumerate(y_copies):
        copy.wait_recv()
        total = total + y_in[n]
    diag_out[...] = pivot[...] - (total[:, :64] + total[:, 64:])

    for copy in sent:
        copy.wait_send()

    @pl.when(jnp.logical_not(stays))
    def _():
        row_copy.wait_send()


def body(ancestor_inverse, lower_panel, pivot_inverse, struct_list):
    vmem = pl.BlockSpec(memory_space=pltpu.VMEM)
    hbm = pl.BlockSpec(memory_space=pltpu.HBM)
    dma = pltpu.SemaphoreType.DMA
    hop_sems = [dma((6 * CHUNKS,))] * 4
    return pl.pallas_call(
        kernel,
        out_shape=(
            jax.ShapeDtypeStruct((768, 64), BF16),
            jax.ShapeDtypeStruct((8, 64), F32),
        ),
        in_specs=[vmem, hbm, hbm, hbm],
        out_specs=(vmem, vmem),
        scratch_shapes=[
            pltpu.VMEM((768, 1536), BF16),
            pltpu.VMEM((8, 64), F32),
            pltpu.VMEM((ROWS, 1024), BF16),
            pltpu.VMEM((ROWS, 1024), BF16),
            pltpu.VMEM((1536, 1024), BF16),
            pltpu.VMEM((ROWS, 1024), BF16),
            pltpu.VMEM((768, B), BF16),
            pltpu.VMEM((4, 2, CHUNKS, CHUNK, B), F32),
            pltpu.VMEM((CHUNKS, 6, CHUNK, B), F32),
            pltpu.VMEM((4, CHUNKS, 2, CHUNK // 2, 128), F32),
            pltpu.VMEM((CHUNKS, 6, CHUNK // 2, 128), F32),
            pltpu.VMEM((2, 2, 8, 8, 128), F32),
            pltpu.VMEM((2, 8, 8, 128), F32),
            pltpu.VMEM((2, 8, 8, 128), F32),
            pltpu.VMEM((15, 8, 128), F32),
            dma((5,)),
            dma((2,)),
            dma((16,)),
            dma((16,)),
            dma((16,)),
            dma((16,)),
            dma((3,)),
            dma((3,)),
            dma((3,)),
            dma((4,)),
            dma((4,)),
            *hop_sems,
            dma((2,)),
            dma((15,)),
            dma((15,)),
        ],
        compiler_params=pltpu.CompilerParams(
            collective_id=0, has_side_effects=True
        ),
    )(struct_list, ancestor_inverse, lower_panel, pivot_inverse)


def solution(mesh):
    placed = (P("pcol", "prow"), P(("prow", "pcol"), None), P("pcol", "prow"), P())
    return jax.shard_map(
        body,
        mesh=mesh,
        in_specs=placed,
        out_specs=(P("pcol", "prow"), P("pcol", "prow")),
        check_vma=False,
    )
```

```python
import jax
import jax.numpy as jnp
from jax import lax
from jax.experimental import pallas as pl
from jax.experimental.pallas import tpu as pltpu
from jax.sharding import PartitionSpec as P

B = 256
NK = 4
MESH = pl.DeviceIdType.MESH
F32 = jnp.float32
BF16 = jnp.bfloat16
ROWS = 48
SHARES = 16
CHUNKS = 2
CHUNK = 384 // CHUNKS


def remote(src, dst, send, recv, device):
    return pltpu.make_async_remote_copy(
        src_ref=src, dst_ref=dst, send_sem=send, recv_sem=recv, device_id=device, device_id_type=MESH
    )


def kernel(
    lists,
    inverse_hbm,
    lower_hbm,
    pivot_hbm,
    off_out,
    diag_out,
    inverse,
    pivot,
    raw,
    lower,
    gathered,
    row_in,
    own_rows,
    part,
    x_in,
    z_part,
    z_in,
    core_part,
    core_in,
    y_part,
    y_in,
    local_sem,
    pair_sem,
    ring_send,
    ring_recv,
    core_send,
    core_recv,
    row_sem,
    slice_send,
    slice_recv,
    band_send,
    band_recv,
    x_send,
    x_recv,
    z_send,
    z_recv,
    sum_sem,
    y_send,
    y_recv,
):
    r, c = lax.axis_index("prow"), lax.axis_index("pcol")
    x, zh = r // 4, r % 4
    zl, y, core = c // 16, (c % 16) // 2, c % 2
    share = zh * 4 + x
    source = {"prow": c // 2, "pcol": (c % 2) * SHARES + share}
    target_row, target_col = (c % 4) * 4 + (c % SHARES) // 4, 2 * r + c // SHARES
    stays = (target_row == r) & (target_col == c)

    def col_device(z_lo, y_at, core_at):
        return {"prow": r, "pcol": z_lo * 16 + (y_at % 8) * 2 + core_at}

    def x_device(step):
        return {"prow": ((x + step + 4) % 4) * 4 + zh, "pcol": c}

    def z_device(step):
        return {"prow": x * 4 + (zh + step + 4) % 4, "pcol": c}

    big_copy = pltpu.make_async_copy(inverse_hbm, inverse, local_sem.at[1])
    big_copy.start()
    pivot_copy = pltpu.make_async_copy(pivot_hbm, pivot, local_sem.at[2])
    pivot_copy.start()

    raw_copy = pltpu.make_async_copy(lower_hbm, raw, local_sem.at[4])
    raw_copy.start()

    barrier = pltpu.get_barrier_semaphore()
    friends = [col_device(zl, y + i, core) for i in range(1, 8)]
    friends += [col_device(1 - zl, y + i, core) for i in range(8)] + [col_device(zl, y, 1 - core)]
    friends += [x_device(1), x_device(2), x_device(3), z_device(1), z_device(-1)]
    for device in friends:
        pl.semaphore_signal(barrier, inc=1, device_id=device, device_id_type=MESH)

    @pl.when(jnp.logical_not(stays))
    def _():
        pl.semaphore_signal(barrier, inc=1, device_id=source, device_id_type=MESH)

    def listed(ancestor):
        found = jnp.where(lists[...] == ancestor, 1.0, 0.0)
        return jnp.max(found, axis=1, keepdims=True)

    raw_copy.wait()
    begin = (r * 32 + c) * ROWS
    first = begin // B
    in_first = lax.broadcasted_iota(jnp.int32, (ROWS, B), 0) + begin < (first + 1) * B
    of_first, of_next = listed(first), listed(first + 1)
    for k in range(NK):
        columns = pl.ds(k * B, B)
        member = jnp.where(in_first, of_first[k : k + 1, :], of_next[k : k + 1, :])
        lower[:, columns] = (raw[:, columns].astype(F32) * member).astype(BF16)

    pl.semaphore_wait(barrier, len(friends) + 1 - stays.astype(jnp.int32))

    def shard(z_lo, y_at, core_at):
        at = (z_lo * 16 + y_at * 2 + core_at) * ROWS
        return gathered.at[pl.ds(pl.multiple_of(at, 16), ROWS)]

    sent = []
    core_copies = []

    def send(src, dst, send_sem, recv_sem, device):
        copy = remote(src, dst, send_sem, recv_sem, device)
        copy.start()
        sent.append(copy)
        return copy

    def to_core(src, dst):
        n = len(core_copies)
        core_copies.append(
            send(src, dst, core_send.at[n], core_recv.at[n], col_device(zl, y, 1 - core))
        )

    ring = {}

    def to_ring(chain, way, step, src, dst):
        n = (chain * 2 + way) * 4 + step
        device = col_device(zl, y + (1 if way == 0 else 7), core)
        ring[chain, way, step] = send(src, dst, ring_send.at[n], ring_recv.at[n], device)

    mine = shard(zl, y, core)
    pair = send(lower, mine, pair_sem.at[0], pair_sem.at[1], col_device(1 - zl, y, core))
    to_ring(0, 0, 0, lower, mine)
    to_ring(0, 1, 0, lower, mine)
    to_core(lower, mine)
    keep = pltpu.make_async_copy(lower, mine, local_sem.at[0])
    keep.start()
    row_copy = remote(
        lower, row_in, row_sem.at[0], row_sem.at[1], {"prow": target_row, "pcol": target_col}
    )
    row_keep = pltpu.make_async_copy(lower, row_in, row_sem.at[2])

    @pl.when(jnp.logical_not(stays))
    def _():
        row_copy.start()

    @pl.when(stays)
    def _():
        row_keep.start()

    pair.wait_recv()
    theirs = shard(1 - zl, y, core)
    to_ring(1, 0, 0, theirs, theirs)
    to_ring(1, 1, 0, theirs, theirs)
    to_core(theirs, theirs)
    for step in range(1, 5):
        for chain in range(2):
            for way in range(2):
                if (chain, way, step - 1) not in ring:
                    continue
                ring[chain, way, step - 1].wait_recv()
                origin = (y + (8 - step if way == 0 else step)) % 8
                piece = shard(zl if chain == 0 else 1 - zl, origin, core)
                if step < 3 or (step == 3 and chain == way):
                    to_ring(chain, way, step, piece, piece)
                to_core(piece, piece)

    def columns_of(k):
        return pl.ds(pl.multiple_of(k * B, B), B)

    def band(at, size):
        return own_rows.at[pl.ds(pl.multiple_of(at, 16), size)]

    @pl.when(jnp.logical_not(stays))
    def _():
        row_copy.wait_recv()

    @pl.when(stays)
    def _():
        row_keep.wait()

    slices = [
        send(
            row_in.at[:, columns_of((x + i) % 4)],
            band(share * ROWS, ROWS),
            slice_send.at[i - 1],
            slice_recv.at[i - 1],
            x_device(i),
        )
        for i in (1, 3, 2)
    ]
    slice_keep = pltpu.make_async_copy(
        row_in.at[:, columns_of(x)], band(share * ROWS, ROWS), local_sem.at[3]
    )
    slice_keep.start()
    keep.wait()
    big_copy.wait()
    for copy in core_copies:
        copy.wait_recv()

    def multiply(k):
        columns = columns_of(k)

        @pl.loop(0, 2)
        def _(half):
            rows = pl.ds(pl.multiple_of(half * 384, 128), 384)
            product = jnp.dot(inverse[rows, :], gathered[:, columns], preferred_element_type=F32)
            part[k, half] = product.reshape(CHUNKS, CHUNK, B)

    def hop(source, target, sends, recvs, chunk, n, device):
        at = chunk * 6 + n
        return send(source, target.at[chunk, n], sends.at[at], recvs.at[at], device)

    far, ahead, behind = (x + 2) % 4, (x + 1) % 4, (x + 3) % 4
    hops = {}

    def x_mid(h):
        hops["x", h, 0] = hop(part.at[far, 0, h], x_in, x_send, x_recv, h, 0, x_device(1))
        hops["x", h, 1] = hop(part.at[far, 1, h], x_in, x_send, x_recv, h, 1, x_device(-1))

    def x_raw_up(h):
        hops["x", h, 2] = hop(part.at[ahead, 1, h], x_in, x_send, x_recv, h, 2, x_device(1))

    def x_raw_down(h):
        hops["x", h, 4] = hop(part.at[behind, 0, h], x_in, x_send, x_recv, h, 4, x_device(-1))

    def x_sum(h):
        hops["x", h, 0].wait_recv()
        part[ahead, 0, h] = part[ahead, 0, h] + x_in[h, 0]
        hops["x", h, 3] = hop(part.at[ahead, 0, h], x_in, x_send, x_recv, h, 3, x_device(1))
        hops["x", h, 1].wait_recv()
        part[behind, 1, h] = part[behind, 1, h] + x_in[h, 1]
        hops["x", h, 5] = hop(part.at[behind, 1, h], x_in, x_send, x_recv, h, 5, x_device(-1))

    z_far, z_ahead, z_behind = (zh + 2) % 4, (zh + 1) % 4, (zh + 3) % 4

    def z_start(h):
        for n in (2, 3, 4, 5):
            hops["x", h, n].wait_recv()
        for way in range(2):
            rows = pl.ds(way * (CHUNK // 2), CHUNK // 2)
            low = part[x, 0, h, rows, :] + x_in[h, 3, rows, :] + x_in[h, 4, rows, :]
            high = part[x, 1, h, rows, :] + x_in[h, 5, rows, :] + x_in[h, 2, rows, :]
            for q in range(4):
                lanes = slice(64 * q, 64 * q + 64)
                z_part[q, h, way] = jnp.concatenate([low[:, lanes], high[:, lanes]], axis=1)
        up, down = z_device(1), z_device(-1)
        hops["z", h, 0] = hop(z_part.at[z_far, h, 0], z_in, z_send, z_recv, h, 0, up)
        hops["z", h, 1] = hop(z_part.at[z_far, h, 1], z_in, z_send, z_recv, h, 1, down)
        hops["z", h, 2] = hop(z_part.at[z_ahead, h, 1], z_in, z_send, z_recv, h, 2, up)
        hops["z", h, 4] = hop(z_part.at[z_behind, h, 0], z_in, z_send, z_recv, h, 4, down)

    def z_sum(h):
        hops["z", h, 0].wait_recv()
        z_part[z_ahead, h, 0] = z_part[z_ahead, h, 0] + z_in[h, 0]
        hops["z", h, 3] = hop(z_part.at[z_ahead, h, 0], z_in, z_send, z_recv, h, 3, z_device(1))
        hops["z", h, 1].wait_recv()
        z_part[z_behind, h, 1] = z_part[z_behind, h, 1] + z_in[h, 1]
        hops["z", h, 5] = hop(z_part.at[z_behind, h, 1], z_in, z_send, z_recv, h, 5, z_device(-1))

    def band_copy(n, at, size, device):
        here = band(at, size)
        return send(here, here, band_send.at[n], band_recv.at[n], device)

    multiply(far)
    x_mid(0)
    multiply(ahead)
    x_raw_up(0)
    multiply(behind)
    x_raw_down(0)
    if CHUNKS > 1:
        x_mid(1)
    slice_keep.wait()
    for copy in slices:
        copy.wait_recv()
    band_up = band_copy(0, zh * 192, 192, z_device(1))
    band_down = band_copy(1, zh * 192, 192, z_device(-1))
    multiply(x)

    for h in range(CHUNKS):
        x_sum(h)
        if h + 1 < CHUNKS:
            x_raw_up(h + 1)
            x_raw_down(h + 1)
        if h + 2 < CHUNKS:
            x_mid(h + 2)
        if h == 0:
            band_up.wait_recv()
            far_up = band_copy(2, z_behind * 192, 96, z_device(1))
            band_down.wait_recv()
            far_down = band_copy(3, z_ahead * 192 + 96, 96, z_device(-1))
        if h >= 2:
            z_sum(h - 2)
        if h >= 1:
            z_start(h - 1)
    if CHUNKS > 1:
        z_sum(CHUNKS - 2)
    z_start(CHUNKS - 1)
    z_sum(CHUNKS - 1)
    far_up.wait_recv()
    far_down.wait_recv()

    half_rows = CHUNK // 2
    lane = lax.broadcasted_iota(jnp.int32, (half_rows, 128), 1)
    row = lax.broadcasted_iota(jnp.int32, (half_rows, 128), 0) + jnp.where(lane < 64, 0, 384)
    kept = [-listed(c * 3 + i) for i in range(3)]
    level = lax.broadcasted_iota(jnp.int32, (NK, 1), 0) == x
    kept = [jnp.sum(jnp.where(level, k, 0.0), axis=0, keepdims=True) for k in kept]
    left_sum = jnp.zeros((B, 128), F32)
    right_sum = jnp.zeros((B, 128), F32)
    over_rows = (((0,), (0,)), ((), ()))
    for h in range(CHUNKS):
        for n in (2, 3, 4, 5):
            hops["z", h, n].wait_recv()
        for way in range(2):
            start = h * CHUNK + way * half_rows
            at = row + start
            keep_row = jnp.where(at < B, kept[0], jnp.where(at < 2 * B, kept[1], kept[2]))
            first, second = (3, 4) if way == 0 else (5, 2)
            total = (z_part[zh, h, way] + z_in[h, first] + z_in[h, second]) * keep_row
            off_out[pl.ds(start, half_rows), :] = total[:, :64].astype(BF16)
            off_out[pl.ds(384 + start, half_rows), :] = total[:, 64:].astype(BF16)
            big = total.astype(BF16)
            small = (total - big.astype(F32)).astype(BF16)
            left = own_rows[pl.ds(start, half_rows), :]
            right = own_rows[pl.ds(384 + start, half_rows), :]
            for piece in (big, small):
                left_sum = left_sum + lax.dot_general(
                    left, piece, over_rows, preferred_element_type=F32
                )
                right_sum = right_sum + lax.dot_general(
                    right, piece, over_rows, preferred_element_type=F32
                )
    lane = lax.broadcasted_iota(jnp.int32, (B, 128), 1)
    term = jnp.where(lane < 64, left_sum, right_sum).reshape(2, 8, 2, 8, 128)

    for q in range(2):
        core_part[q] = term[:, :, q]
    copy = send(
        core_part.at[1 - core], core_in, sum_sem.at[0], sum_sem.at[1], col_device(zl, y, 1 - core)
    )
    copy.wait_recv()
    y_part[...] = core_part[core] + core_in[...]
    y_copies = []
    for n in range(1, 16):
        z_to, y_to = (zl + n // 8) % 2, (y + n) % 8
        y_copies.append(
            send(
                y_part.at[z_to, y_to],
                y_in.at[n - 1],
                y_send.at[n - 1],
                y_recv.at[n - 1],
                col_device(z_to, y_to, core),
            )
        )
    pivot_copy.wait()
    total = y_part[zl, y]
    for n, copy in enumerate(y_copies):
        copy.wait_recv()
        total = total + y_in[n]
    diag_out[...] = pivot[...] - (total[:, :64] + total[:, 64:])

    for copy in sent:
        copy.wait_send()

    @pl.when(jnp.logical_not(stays))
    def _():
        row_copy.wait_send()


def body(ancestor_inverse, lower_panel, pivot_inverse, struct_list):
    vmem = pl.BlockSpec(memory_space=pltpu.VMEM)
    hbm = pl.BlockSpec(memory_space=pltpu.HBM)
    dma = pltpu.SemaphoreType.DMA
    hop_sems = [dma((6 * CHUNKS,))] * 4
    return pl.pallas_call(
        kernel,
        out_shape=(
            jax.ShapeDtypeStruct((768, 64), BF16),
            jax.ShapeDtypeStruct((8, 64), F32),
        ),
        in_specs=[vmem, hbm, hbm, hbm],
        out_specs=(vmem, vmem),
        scratch_shapes=[
            pltpu.VMEM((768, 1536), BF16),
            pltpu.VMEM((8, 64), F32),
            pltpu.VMEM((ROWS, 1024), BF16),
            pltpu.VMEM((ROWS, 1024), BF16),
            pltpu.VMEM((1536, 1024), BF16),
            pltpu.VMEM((ROWS, 1024), BF16),
            pltpu.VMEM((768, B), BF16),
            pltpu.VMEM((4, 2, CHUNKS, CHUNK, B), F32),
            pltpu.VMEM((CHUNKS, 6, CHUNK, B), F32),
            pltpu.VMEM((4, CHUNKS, 2, CHUNK // 2, 128), F32),
            pltpu.VMEM((CHUNKS, 6, CHUNK // 2, 128), F32),
            pltpu.VMEM((2, 2, 8, 8, 128), F32),
            pltpu.VMEM((2, 8, 8, 128), F32),
            pltpu.VMEM((2, 8, 8, 128), F32),
            pltpu.VMEM((15, 8, 128), F32),
            dma((5,)),
            dma((2,)),
            dma((16,)),
            dma((16,)),
            dma((16,)),
            dma((16,)),
            dma((3,)),
            dma((3,)),
            dma((3,)),
            dma((4,)),
            dma((4,)),
            *hop_sems,
            dma((2,)),
            dma((15,)),
            dma((15,)),
        ],
        compiler_params=pltpu.CompilerParams(
            collective_id=0, has_side_effects=True
        ),
    )(struct_list, ancestor_inverse, lower_panel, pivot_inverse)


def solution(mesh):
    placed = (P("pcol", "prow"), P(("prow", "pcol"), None), P("pcol", "prow"), P())
    return jax.shard_map(
        body,
        mesh=mesh,
        in_specs=placed,
        out_specs=(P("pcol", "prow"), P("pcol", "prow")),
        check_vma=False,
    )
```
